32 devices in a mesh: row: 8 (over y, x, core), col: 4 (over z).
Axes of the slice: x: 2, y: 2, z: 4, core: 2. Of those that a mesh axis runs over, the one named last changes fastest.
Arguments:
- front_init: float32 [16384, 16384], P('row', 'col'), as said below
- child_tiles: bfloat16 [1024, 256, 256], P(('row', 'col'))
- child_dest: int32 [1024], P(('row', 'col')), may hold values from 0 to 4095, as said below
Outputs:
- panel_factor: float32 [16384, 1024], P('row')
- schur_update: float32 [16384, 16384], P('row', 'col')
The draws below stay inside these ranges and needn't reach their ends.
Inputs may be any that keep to these rules, and one draw needn't show every extreme that they name: `child_dest`: t = 64 * tile row + tile column. A tile held at col index c has its tile column in c * 16 to (c + 1) * 16 - 1. Of one device's tiles at most 4 have tile rows in one block of 8 tile rows, and in every column of the mesh one such block gets exactly 4 from every device of that column. The leading 1024 x 1024 block of front_init plus any child tiles added to it is strictly diagonally dominant.
All inputs are finite; a program needn't handle non-finite values.
Results may differ from the reference program's by a relative error of at most 0.0003.
Values may be sent and summed in bfloat16 or wider, within the bound.
No kernel may reach another device: no remote copies, remote signals or barrier semaphores. Data moves between devices by JAX's collectives and lax.ppermute only.
A program may use at most 256 MiB of HBM per device.

```python
import jax
import jax.numpy as jnp
from jax import lax

NF = 16384
PW = 1024
TW = 256
CAP = 4
CTD = 32
NT = 64
TRD = 8
TCD = 16
NCHILD = 1024


def route_tiles(key):
    base_key = jax.random.fold_in(key, 11)
    row_count = NF // (TRD * TW)
    col_count = NF // (TCD * TW)
    device_count = row_count * col_count
    hot_key, perm_key, order_key, row_key, col_key = jax.random.split(base_key, 5)
    hot_rows = jax.random.randint(hot_key, (col_count,), 0, row_count)
    device_col = jnp.arange(device_count) % col_count
    hot_device = hot_rows[device_col]
    other_slots = (row_count - 1) * CAP
    perm_keys = jax.random.split(perm_key, device_count)
    perms = jax.vmap(lambda sub_key: jax.random.permutation(sub_key, other_slots))(perm_keys)
    picked = perms[:, :CTD - CAP] // CAP
    picked = picked + (picked >= hot_device[:, None]).astype(jnp.int32)
    hot_block = jnp.broadcast_to(hot_device[:, None], (device_count, CAP))
    owners = jnp.concatenate([hot_block, picked], axis=1).astype(jnp.int32)
    order_keys = jax.random.split(order_key, device_count)
    shuffle = jax.vmap(lambda sub_key: jax.random.permutation(sub_key, CTD))(order_keys)
    owners = jnp.take_along_axis(owners, shuffle, axis=1)
    tile_row = owners * TRD + jax.random.randint(row_key, (device_count, CTD), 0, TRD)
    tile_col = device_col[:, None] * TCD + jax.random.randint(col_key, (device_count, CTD), 0, TCD)
    return (tile_row * NT + tile_col).reshape(-1).astype(jnp.int32)


def draw_child_dest(key, part):
    return route_tiles(key)


def draw_child_tiles(key, part):
    targets = route_tiles(key)
    pivot_tiles = PW // TW
    target_row = targets // NT
    target_col = targets % NT
    in_pivot = (target_row < pivot_tiles) & (target_col < pivot_tiles)
    pivot_ids = jnp.arange(pivot_tiles, dtype=jnp.int32)
    row_match = target_row[:, None] == pivot_ids[None, :]
    col_match = target_col[:, None] == pivot_ids[None, :]
    row_hits = jnp.sum((row_match & in_pivot[:, None]).astype(jnp.int32), axis=0)
    col_hits = jnp.sum((col_match & in_pivot[:, None]).astype(jnp.int32), axis=0)
    row_crowd = jnp.sum(jnp.where(row_match, row_hits[None, :], 0), axis=1)
    col_crowd = jnp.sum(jnp.where(col_match, col_hits[None, :], 0), axis=1)
    crowding = jnp.maximum(jnp.maximum(row_crowd, col_crowd), 1).astype(jnp.float32)
    values = jax.random.uniform(jax.random.fold_in(key, 5), (NCHILD, TW, TW), jnp.float32, -0.5, 0.5)
    tile_scale = jax.random.uniform(jax.random.fold_in(key, 7), (NCHILD,), jnp.float32, 0.2, 1.0)
    positive = (values + 0.5) * tile_scale[:, None, None]
    chosen = jnp.where(in_pivot[:, None, None], positive, values)
    factor = jnp.where(in_pivot, 0.5 / (TW * crowding), 1.0).astype(jnp.float32)
    return (chosen * factor[:, None, None]).astype(jnp.bfloat16)


def draw_front_init(key, part):
    unit = jax.random.uniform(jax.random.fold_in(key, 3), (NF, NF), jnp.float32)
    signed = 2.0 * unit - 1.0
    row_ids = jax.lax.broadcasted_iota(jnp.int32, (NF, NF), 0)
    col_ids = jax.lax.broadcasted_iota(jnp.int32, (NF, NF), 1)
    amplitude = 2.42 * PW ** (-0.25)
    root_width = PW ** 0.5
    diag_value = jnp.where(row_ids < PW, 2.6 + 2.6 * unit, root_width * (1.25 + 1.25 * unit))
    both_pivot = (row_ids < PW) & (col_ids < PW)
    either_pivot = (row_ids < PW) | (col_ids < PW)
    neighbour = jnp.abs(row_ids - col_ids) == 1
    pivot_off = jnp.where(neighbour, -(0.4 + 0.4 * unit), unit * (0.4 / PW))
    off_value = jnp.where(both_pivot, pivot_off, jnp.where(either_pivot, signed * amplitude, signed))
    return jnp.where(row_ids == col_ids, diag_value, off_value).astype(jnp.float32)


def setup_inputs(seed: int = 0) -> dict:
    key_of = jax.random.split(jax.random.key(seed), 4)
    front_init = draw_front_init(jax.random.fold_in(key_of[3], 71), 0)
    child_tiles = draw_child_tiles(jax.random.fold_in(key_of[3], 71), 0)
    child_dest = draw_child_dest(jax.random.fold_in(key_of[3], 71), 0)
    return {"front_init": front_init, "child_tiles": child_tiles, "child_dest": child_dest}


def reference(front_init, child_tiles, child_dest):
    tile_sums = jnp.zeros((NT * NT, TW, TW), jnp.float32).at[child_dest].add(child_tiles.astype(jnp.float32))
    added_tiles = tile_sums.reshape(NT, NT, TW, TW).transpose(0, 2, 1, 3).reshape(NF, NF)
    front_sum = front_init + added_tiles
    column_panel = front_sum[:, :PW]
    pivot_raw = column_panel[:PW]
    pivot_sym = (pivot_raw + pivot_raw.T) * 0.5
    pivot_factor = jnp.linalg.cholesky(pivot_sym)
    panel_factor = jax.scipy.linalg.solve_triangular(pivot_factor, column_panel.T, lower=True).T
    schur_update = front_sum - jnp.dot(panel_factor.astype(jnp.float32), panel_factor.T.astype(jnp.float32), precision=lax.Precision.HIGHEST, preferred_element_type=jnp.float32)
    return (panel_factor, schur_update)
```

```python
import functools

import jax
import jax.numpy as jnp
from jax import lax
from jax.experimental import pallas as pl
from jax.experimental.pallas import tpu as pltpu
from jax.sharding import PartitionSpec as P

PW = 1024
CAP = 4
BLK = 128
KP = 256
GRP = 256
EXT = 16
CODE = 64.0
TOP = 32767.0
HI = lax.Precision.HIGHEST
F32 = jnp.float32
ANY = pl.BlockSpec(memory_space=pl.ANY)
VMEM_CAP = 58 << 20


def params(limit=VMEM_CAP):
    return pltpu.CompilerParams(vmem_limit_bytes=limit)


def dot_t(a, b, precision=HI):
    return lax.dot_general(
        a, b, (((1,), (1,)), ((), ())), precision=precision, preferred_element_type=F32
    )


def pack_kernel(idx_ref, src_ref, out_ref, held, sem_in, sem_out):
    slots = out_ref.shape[0]

    def fetch(s):
        return pltpu.make_async_copy(src_ref.at[idx_ref[s]], held.at[s], sem_in.at[s])

    def flush(s):
        return pltpu.make_async_copy(held.at[s], out_ref.at[s], sem_out.at[s])

    for s in range(slots):
        fetch(s).start()
    for s in range(slots):
        fetch(s).wait()
        flush(s).start()
    for s in range(slots):
        flush(s).wait()


def pack(index, tiles):
    slots = index.shape[0]
    shape = (slots,) + tiles.shape[1:]
    return pl.pallas_call(
        pack_kernel,
        out_shape=jax.ShapeDtypeStruct(shape, tiles.dtype),
        grid_spec=pltpu.PrefetchScalarGridSpec(
            num_scalar_prefetch=1,
            grid=(1,),
            in_specs=[ANY],
            out_specs=ANY,
            scratch_shapes=[
                pltpu.VMEM(shape, tiles.dtype),
                pltpu.SemaphoreType.DMA((slots,)),
                pltpu.SemaphoreType.DMA((slots,)),
            ],
        ),
        compiler_params=params(),
        name="pack",
    )(index, tiles)


PARTS = 4


def pick_kernel(idx_ref, *refs):
    sources, (out_ref, held, sem_in, sem_out) = refs[:-4], refs[-4:]
    step = out_ref.shape[0] // PARTS
    for i, source in enumerate(sources):

        @pl.when(idx_ref[0] == i)
        def _(source=source):
            for p in range(PARTS):
                at = pl.ds(p * step, step)
                pltpu.make_async_copy(source.at[at], held.at[at], sem_in.at[p]).start()

    flushes = []
    for p in range(PARTS):
        at = pl.ds(p * step, step)
        pltpu.make_async_copy(sources[0].at[at], held.at[at], sem_in.at[p]).wait()
        flush = pltpu.make_async_copy(held.at[at], out_ref.at[at], sem_out.at[p])
        flush.start()
        flushes.append(flush)
    for flush in flushes:
        flush.wait()


def pick(which, arrays):
    shape, dtype = arrays[0].shape, arrays[0].dtype
    return pl.pallas_call(
        pick_kernel,
        out_shape=jax.ShapeDtypeStruct(shape, dtype),
        grid_spec=pltpu.PrefetchScalarGridSpec(
            num_scalar_prefetch=1,
            grid=(1,),
            in_specs=[ANY] * len(arrays),
            out_specs=ANY,
            scratch_shapes=[
                pltpu.VMEM(shape, dtype),
                pltpu.SemaphoreType.DMA((PARTS,)),
                pltpu.SemaphoreType.DMA((PARTS,)),
            ],
        ),
        compiler_params=params(),
        name="pick",
    )(which.reshape(1).astype(jnp.int32), *arrays)


def add_tiles(rows_ref, cols_ref, tiles_ref, out_ref, row0, col0):
    tile = tiles_ref.shape[1]
    high, wide = out_ref.shape[0] // tile, out_ref.shape[1] // tile

    def step(t, carry):
        row = rows_ref[t] - row0
        col = cols_ref[t] - col0

        @pl.when((row >= 0) & (row < high) & (col >= 0) & (col < wide))
        def _():
            at = pl.ds(pl.multiple_of(row * tile, tile), tile)
            to = pl.ds(pl.multiple_of(col * tile, tile), tile)
            out_ref[at, to] += tiles_ref[t].astype(F32)

        return carry

    lax.fori_loop(0, tiles_ref.shape[0], step, 0)


def panel_kernel(rows_ref, cols_ref, front_ref, tiles_ref, out_ref):
    out_ref[...] = front_ref[...]
    high = out_ref.shape[0] // tiles_ref.shape[1]
    add_tiles(rows_ref, cols_ref, tiles_ref, out_ref, pl.program_id(0) * high, 0)


def panel(place_rows, place_cols, front, tiles):
    rows = front.shape[0]
    high = min(rows, 512)
    return pl.pallas_call(
        panel_kernel,
        out_shape=jax.ShapeDtypeStruct((rows, PW), F32),
        grid_spec=pltpu.PrefetchScalarGridSpec(
            num_scalar_prefetch=2,
            grid=(rows // high,),
            in_specs=[
                pl.BlockSpec((high, PW), lambda i, r, c: (i, 0)),
                pl.BlockSpec(tiles.shape, lambda i, r, c: (0, 0, 0), pipeline_mode=pl.Buffered(1)),
            ],
            out_specs=pl.BlockSpec((high, PW), lambda i, r, c: (i, 0)),
        ),
        compiler_params=params(),
        name="panel",
    )(place_rows, place_cols, front, tiles)


def spread(x, s):
    return jnp.broadcast_to(x[s : s + 1, :], x.shape)


def factor_block(sym):
    groups = BLK // 8
    rows = [sym[8 * v : 8 * v + 8, :] for v in range(groups)]
    lane = lax.broadcasted_iota(jnp.int32, (8, BLK), 1)
    sub = lax.broadcasted_iota(jnp.int32, (8, BLK), 0)
    for v0 in range(groups):
        first = 8 * v0
        cur = rows[v0]
        cols = [jnp.broadcast_to(cur[:, first + k : first + k + 1], (8, BLK)) for k in range(8)]
        scaled, mults = [], []
        for jj in range(8):
            at = lane == first + jj
            below = sub > jj
            inv = 1.0 / spread(cols[jj], jj)
            rs = jnp.where(at, inv, spread(cur, jj) * inv)
            mult = [None if k <= jj else spread(cols[k], jj) * inv for k in range(8)]
            f = jnp.where(below, cols[jj], 0.0)
            cur = jnp.where(at & below, 0.0, cur) - f * rs
            for k in range(jj + 1, 8):
                cols[k] = cols[k] - f * mult[k]
            scaled.append(jnp.where((lane > first + jj) & (lane < first + 8), 0.0, rs))
            mults.append(mult)
        rows[v0] = cur
        inside = (lane >= first) & (lane < first + 8)
        for v in range(v0 + 1, groups):
            cols = [
                jnp.broadcast_to(rows[v][:, first + k : first + k + 1], (8, BLK))
                for k in range(8)
            ]
            new = jnp.where(inside, 0.0, rows[v])
            for jj in range(8):
                new = new - cols[jj] * scaled[jj]
                for k in range(jj + 1, 8):
                    cols[k] = cols[k] - cols[jj] * mults[jj][k]
            rows[v] = new
    return jnp.concatenate(rows, axis=0)


def inverse_block(sym):
    done = factor_block(sym)
    row = lax.broadcasted_iota(jnp.int32, (BLK, BLK), 0)
    col = lax.broadcasted_iota(jnp.int32, (BLK, BLK), 1)
    diag = jnp.sum(jnp.where(row == col, done, 0.0), axis=1, keepdims=True)
    unit = jnp.where(row > col, done, jnp.where(row == col, 1.0, 0.0))
    return unit * lax.rsqrt(diag)


def chol_kernel(a_ref, l_ref, *rest, symmetrize):
    trail_ref = rest[0] if len(rest) == 2 else None
    work = rest[-1]
    n = work.shape[0]
    if symmetrize:
        for i in range(n // KP):
            for j in range(i + 1):
                si, sj = pl.ds(i * KP, KP), pl.ds(j * KP, KP)
                work[si, sj] = (a_ref[si, sj] + a_ref[sj, si].T) * 0.5
    else:
        work[...] = a_ref[...]

    def step(b, carry):
        r0 = pl.multiple_of(b * BLK, BLK)
        inv = inverse_block(work[pl.ds(r0, BLK), pl.ds(r0, BLK)])
        l_ref[pl.ds(r0, BLK), pl.ds(r0, BLK)] = inv

        @pl.when(b == 0)
        def _():
            l_ref[0:BLK, BLK:KP] = jnp.zeros((BLK, KP - BLK), F32)
            low = dot_t(work[BLK:n, 0:BLK], inv)
            l_ref[BLK:n, 0:BLK] = low
            work[BLK:n, BLK:KP] -= dot_t(low, low[0:BLK])

        @pl.when(b == 1)
        def _():
            side = jnp.dot(
                l_ref[BLK:KP, 0:BLK], l_ref[0:BLK, 0:BLK], precision=HI, preferred_element_type=F32
            )
            l_ref[BLK:KP, 0:BLK] = -jnp.dot(inv, side, precision=HI, preferred_element_type=F32)
            if n > KP:
                l_ref[KP:n, BLK:KP] = dot_t(work[KP:n, BLK:KP], inv)

        return carry

    lax.fori_loop(0, KP // BLK, step, 0)
    if trail_ref is not None:
        m = n - KP
        for j in range(m // KP):
            rows = slice(j * KP, m)
            cols = slice(j * KP, (j + 1) * KP)
            low = l_ref[KP + j * KP : n, :]
            trail_ref[rows, cols] = work[KP + j * KP : n, KP + j * KP : KP + (j + 1) * KP] - dot_t(
                low, low[0:KP]
            )


def chol_step(a, symmetrize):
    n = PW if symmetrize else a.shape[0]
    shapes = [jax.ShapeDtypeStruct((n, KP), F32)]
    whole = lambda shape: pl.BlockSpec(shape, lambda i: (0,) * len(shape))
    if n > KP:
        shapes.append(jax.ShapeDtypeStruct((n - KP, n - KP), F32))
    return pl.pallas_call(
        functools.partial(chol_kernel, symmetrize=symmetrize),
        out_shape=shapes,
        grid=(1,),
        in_specs=[whole((n, n))],
        out_specs=[whole(s.shape) for s in shapes],
        scratch_shapes=[pltpu.VMEM((n, n), F32)],
        compiler_params=params(),
        name="chol",
    )(a)


def eye(n):
    return lax.broadcasted_iota(jnp.int32, (n, n), 0) == lax.broadcasted_iota(jnp.int32, (n, n), 1)


def solve_kernel(p_ref, *refs, k):
    factors, lowers = refs[:k], refs[k : 2 * k + 1]
    f_ref, q_ref = refs[2 * k + 1 :]
    for g in range(q_ref.shape[0]):
        at = slice(g * GRP, (g + 1) * GRP)
        acc = p_ref[at, :]
        for j in range(k):
            acc = acc - dot_t(factors[j][at, :], lowers[j][(k - j) * KP : (k - j + 1) * KP, :])
        f = dot_t(acc, lowers[k][0:KP, :])
        f_ref[at, :] = f
        peak = jnp.maximum(jnp.max(jnp.abs(f), axis=1, keepdims=True), 1e-30)
        code = jnp.ceil(jnp.log2(peak) * CODE)
        q = jnp.clip(jnp.round(f * (jnp.exp2(code * (-1.0 / CODE)) * TOP)), -TOP, TOP)
        q_ref[g, 0:GRP, :] = q.astype(jnp.int32).astype(jnp.int16)
        codes = jnp.sum(jnp.where(eye(GRP), code, 0.0), axis=0, keepdims=True)
        codes = jnp.broadcast_to(codes, (EXT, GRP))
        q_ref[g, GRP : GRP + EXT, :] = codes.astype(jnp.int32).astype(jnp.int16)


def solve(panel_sum, factors, lowers):
    k = len(factors)
    rows = panel_sum.shape[0]
    high = min(rows, 4 * GRP)
    block = pl.BlockSpec((high, KP), lambda i: (i, 0))
    return pl.pallas_call(
        functools.partial(solve_kernel, k=k),
        out_shape=[
            jax.ShapeDtypeStruct((rows, KP), F32),
            jax.ShapeDtypeStruct((rows // GRP, GRP + EXT, KP), jnp.int16),
        ],
        grid=(rows // high,),
        in_specs=[pl.BlockSpec((high, KP), lambda i: (i, k))]
        + [block] * k
        + [pl.BlockSpec(low.shape, lambda i: (0, 0)) for low in lowers],
        out_specs=[block, pl.BlockSpec((high // GRP, GRP + EXT, KP), lambda i: (i, 0, 0))],
        compiler_params=params(),
        name="solve",
    )(panel_sum, *factors, *lowers)


def decode(q_ref, g):
    codes = q_ref[g, GRP : GRP + EXT, :].astype(jnp.int32).astype(F32)[0:1, :]
    code = jnp.sum(jnp.where(eye(GRP), codes, 0.0), axis=1, keepdims=True)
    scale = jnp.exp2(code * (1.0 / CODE)) * (1.0 / TOP)
    return q_ref[g, 0:GRP, :].astype(jnp.int32).astype(F32) * scale


def halves(x):
    high = x.astype(jnp.bfloat16)
    return high, (x - high.astype(F32)).astype(jnp.bfloat16)


def schur_kernel(rows_ref, cols_ref, member_ref, front_ref, tiles_ref, *refs, count):
    own, mine, other = refs[:count], refs[count : 2 * count], refs[2 * count : 3 * count]
    f_ref, out_ref, fh_ref, fl_ref, sh_ref, sl_ref = refs[3 * count :]
    i, j = pl.program_id(0), pl.program_id(1)
    groups = mine[0].shape[0]
    tile = tiles_ref.shape[1]

    @pl.when((i == 0) & (j == 0))
    def _():
        def step(g, carry):
            for e, strip in enumerate((mine, other)):
                member = member_ref[0] if e == 0 else 1 - member_ref[0]
                at = pl.ds(pl.multiple_of((member * groups + g) * GRP, GRP), GRP)
                for k in range(count):
                    high, low = halves(decode(strip[k], g))
                    sh_ref[at, k * KP : (k + 1) * KP] = high
                    sl_ref[at, k * KP : (k + 1) * KP] = low
            return carry

        lax.fori_loop(0, groups, step, 0)

    @pl.when(j == 0)
    def _():
        def step(g, carry):
            at = pl.ds(pl.multiple_of(g * GRP, GRP), GRP)
            for k in range(count):
                f = decode(own[k], g)
                f_ref[at, k * KP : (k + 1) * KP] = f
                high, low = halves(f)
                fh_ref[at, k * KP : (k + 1) * KP] = high
                fl_ref[at, k * KP : (k + 1) * KP] = low
            return carry

        lax.fori_loop(0, own[0].shape[0], step, 0)

    high, wide = out_ref.shape
    at = pl.ds(pl.multiple_of(j * wide, wide), wide)
    fh, fl, sh, sl = fh_ref[...], fl_ref[...], sh_ref[at, :], sl_ref[at, :]
    out_ref[...] = front_ref[...] - (dot_t(fh, sh, None) + (dot_t(fh, sl, None) + dot_t(fl, sh, None)))
    add_tiles(rows_ref, cols_ref, tiles_ref, out_ref, i * (high // tile), j * (wide // tile))


def schur(place_rows, place_cols, member, front, tiles, own, mine, other):
    rows, cols = front.shape
    count = len(own)
    once = pl.Buffered(1)
    high, wide = min(rows, 1024), min(cols, 512)
    depth = count * KP
    block = pl.BlockSpec((high, wide), lambda i, j, *_: (i, j))
    coded = pl.BlockSpec((high // GRP, GRP + EXT, KP), lambda i, j, *_: (i, 0, 0))
    strip = pl.BlockSpec(mine[0].shape, lambda i, j, *_: (0, 0, 0), pipeline_mode=once)
    return pl.pallas_call(
        functools.partial(schur_kernel, count=count),
        out_shape=[jax.ShapeDtypeStruct((rows, PW), F32), jax.ShapeDtypeStruct((rows, cols), F32)],
        grid_spec=pltpu.PrefetchScalarGridSpec(
            num_scalar_prefetch=3,
            grid=(rows // high, cols // wide),
            in_specs=[block, pl.BlockSpec(tiles.shape, lambda i, j, *_: (0, 0, 0), pipeline_mode=once)]
            + [coded] * count
            + [strip] * (2 * count),
            out_specs=[pl.BlockSpec((high, depth), lambda i, j, *_: (i, 0)), block],
            scratch_shapes=[pltpu.VMEM((high, depth), jnp.bfloat16)] * 2
            + [pltpu.VMEM((cols, depth), jnp.bfloat16)] * 2,
        ),
        compiler_params=params(),
        name="schur",
    )(place_rows, place_cols, member, front, tiles, *own, *mine, *other)


def gray(n):
    return [i ^ (i >> 1) for i in range(n)]


def ring_pairs(row_count, col_count, hop):
    chips = row_count // 2
    order = gray(chips)
    pairs = []
    for col in range(col_count):
        at = order.index(col)
        for member in range(2):
            way = 1 if member == 0 else -1
            src = order[(at + way * (hop - 1)) % chips] * 2 + member
            dst = order[(at + way * hop) % chips] * 2 + member
            pairs.append((src * col_count + col, dst * col_count + col))
    return pairs


def body(front_init, child_tiles, child_dest):
    row_count = lax.axis_size("row")
    col_count = lax.axis_size("col")
    if row_count != 2 * col_count:
        raise ValueError("mesh shape")
    row_extent, col_extent = front_init.shape
    tile_width = child_tiles.shape[1]
    tile_grid = col_extent * col_count // tile_width
    row_tiles = row_extent // tile_width
    col_tiles = col_extent // tile_width
    tile_count = child_tiles.shape[0]
    row_index = lax.axis_index("row")
    col_index = lax.axis_index("col")

    tile_row = child_dest // tile_grid
    tile_col = child_dest % tile_grid
    owner_row = tile_row // row_tiles
    local_tile = (tile_row - owner_row * row_tiles) * col_tiles + (tile_col - col_index * col_tiles)
    positions = jnp.arange(tile_count)
    earlier = positions[None, :] < positions[:, None]
    same_owner = owner_row[:, None] == owner_row[None, :]
    send_rank = jnp.sum((same_owner & earlier).astype(jnp.int32), axis=1)
    send_slot = owner_row * CAP + send_rank
    slots = jnp.arange(row_count * CAP)
    hit = slots[:, None] == send_slot[None, :]
    index = jnp.sum(jnp.where(hit, positions[None, :], 0), axis=1).astype(jnp.int32)
    targets = jnp.sum(jnp.where(hit, local_tile[None, :] + 1, 0), axis=1).astype(jnp.int32) - 1
    outgoing = pack(index, child_tiles)
    arrived = lax.all_to_all(outgoing, "row", split_axis=0, concat_axis=0, tiled=True)
    places = lax.all_to_all(targets, "row", split_axis=0, concat_axis=0, tiled=True)

    place_rows = jnp.where(places < 0, -1, places // col_tiles)
    place_cols = places % col_tiles
    panel_sum = panel(place_rows, place_cols, front_init, arrived)

    both = ("row", "col")
    chips = row_count // 2
    member = row_index % 2
    order = jnp.array(gray(chips))
    here = jnp.argmax(order == row_index // 2)
    there = jnp.argmax(order == col_index)
    distance = jnp.where(member == 0, here - there, there - here) % chips
    swap = [(r * col_count + c, (r ^ 1) * col_count + c) for r in range(row_count) for c in range(col_count)]

    def share(low):
        held = [low]
        for chip in range(1, chips):
            parent = chip - (1 << (chip.bit_length() - 1))
            pair = (2 * parent * col_count, 2 * chip * col_count)
            held.append(lax.ppermute(held[parent], both, [pair]))
        even = pick(row_index // 2, held)
        odd = lax.ppermute(even, both, [(2 * c * col_count, (2 * c + 1) * col_count) for c in range(chips)])
        return pick(member, [even, odd])

    count = PW // KP
    pivot = panel_sum
    own, mine, other, factors, lowers = [], [], [], [], []

    def send(k):
        factor, coded = solve(panel_sum, factors, lowers[: k + 1])
        factors.append(factor)
        steps = [coded]
        for hop in range(col_count - 1):
            steps.append(lax.ppermute(steps[-1], "col", [(hop, hop + 1)]))
        own.append(pick(col_index, steps))
        steps = [own[-1]]
        for hop in range(1, chips):
            steps.append(lax.ppermute(steps[-1], both, ring_pairs(row_count, col_count, hop)))
        mine.append(pick(distance, steps))
        other.append(lax.ppermute(mine[-1], both, swap))

    for k in range(count):
        if k == count - 1:
            send(0)
            pivot, factors[0] = lax.optimization_barrier((pivot, factors[0]))
        result = chol_step(pivot, k == 0)
        lowers.append(share(result[0]))
        if k + 1 < count:
            pivot = result[1]
    for k in range(1, count):
        send(k)

    panel_factor, schur_update = schur(
        place_rows, place_cols, member.reshape(1).astype(jnp.int32), front_init, arrived, own, mine, other
    )
    return (panel_factor, schur_update)


def solution(mesh):
    return jax.shard_map(
        body,
        mesh=mesh,
        in_specs=(P("row", "col"), P(("row", "col"), None, None), P(("row", "col"))),
        out_specs=(P("row", None), P("row", "col")),
        check_vma=False,
    )
```

```python
import functools

import jax
import jax.numpy as jnp
from jax import lax
from jax.experimental import pallas as pl
from jax.experimental.pallas import tpu as pltpu
from jax.sharding import PartitionSpec as P


PW = 1024
CAP = 4
BLK = 128
KP = 256
GRP = 256
EXT = 16
CODE = 64.0
TOP = 32767.0
HI = lax.Precision.HIGHEST
F32 = jnp.float32
ANY = pl.BlockSpec(memory_space=pl.ANY)
VMEM_CAP = 58 << 20


def params(limit=VMEM_CAP):
    return pltpu.CompilerParams(vmem_limit_bytes=limit)


def dot_t(a, b, precision=HI):
    return lax.dot_general(
        a, b, (((1,), (1,)), ((), ())), precision=precision, preferred_element_type=F32
    )


def pack_kernel(idx_ref, src_ref, out_ref, held, sem_in, sem_out):
    slots = out_ref.shape[0]

    def fetch(s):
        return pltpu.make_async_copy(src_ref.at[idx_ref[s]], held.at[s], sem_in.at[s])

    def flush(s):
        return pltpu.make_async_copy(held.at[s], out_ref.at[s], sem_out.at[s])

    for s in range(slots):
        fetch(s).start()
    for s in range(slots):
        fetch(s).wait()
        flush(s).start()
    for s in range(slots):
        flush(s).wait()


def pack(index, tiles):
    slots = index.shape[0]
    shape = (slots,) + tiles.shape[1:]
    return pl.pallas_call(
        pack_kernel,
        out_shape=jax.ShapeDtypeStruct(shape, tiles.dtype),
        grid_spec=pltpu.PrefetchScalarGridSpec(
            num_scalar_prefetch=1,
            grid=(1,),
            in_specs=[ANY],
            out_specs=ANY,
            scratch_shapes=[
                pltpu.VMEM(shape, tiles.dtype),
                pltpu.SemaphoreType.DMA((slots,)),
                pltpu.SemaphoreType.DMA((slots,)),
            ],
        ),
        compiler_params=params(),
        name="pack",
    )(index, tiles)


PARTS = 4


def pick_kernel(idx_ref, *refs):
    sources, (out_ref, held, sem_in, sem_out) = refs[:-4], refs[-4:]
    step = out_ref.shape[0] // PARTS
    for i, source in enumerate(sources):

        @pl.when(idx_ref[0] == i)
        def _(source=source):
            for p in range(PARTS):
                at = pl.ds(p * step, step)
                pltpu.make_async_copy(source.at[at], held.at[at], sem_in.at[p]).start()

    flushes = []
    for p in range(PARTS):
        at = pl.ds(p * step, step)
        pltpu.make_async_copy(sources[0].at[at], held.at[at], sem_in.at[p]).wait()
        flush = pltpu.make_async_copy(held.at[at], out_ref.at[at], sem_out.at[p])
        flush.start()
        flushes.append(flush)
    for flush in flushes:
        flush.wait()


def pick(which, arrays):
    shape, dtype = arrays[0].shape, arrays[0].dtype
    return pl.pallas_call(
        pick_kernel,
        out_shape=jax.ShapeDtypeStruct(shape, dtype),
        grid_spec=pltpu.PrefetchScalarGridSpec(
            num_scalar_prefetch=1,
            grid=(1,),
            in_specs=[ANY] * len(arrays),
            out_specs=ANY,
            scratch_shapes=[
                pltpu.VMEM(shape, dtype),
                pltpu.SemaphoreType.DMA((PARTS,)),
                pltpu.SemaphoreType.DMA((PARTS,)),
            ],
        ),
        compiler_params=params(),
        name="pick",
    )(which.reshape(1).astype(jnp.int32), *arrays)


def bucket(rows, cols, high, wide, row_blocks, col_blocks):
    count = rows.shape[0]
    inside = (rows >= 0) & (cols < wide * col_blocks)
    key = jnp.where(inside, (rows // high) * col_blocks + cols // wide, row_blocks * col_blocks)
    at = jnp.arange(count)
    before = (key[None, :] < key[:, None]) | ((key[None, :] == key[:, None]) & (at[None, :] < at[:, None]))
    place = jnp.sum(before.astype(jnp.int32), axis=1)
    order = jnp.sum(jnp.where(place[None, :] == at[:, None], at[None, :], 0), axis=1).astype(jnp.int32)
    edges = jnp.arange(row_blocks * col_blocks + 1)
    starts = jnp.sum((key[None, :] < edges[:, None]).astype(jnp.int32), axis=1)
    return order, starts


def add_tiles(scalars, tiles_ref, out_ref, block, row0, col0):
    rows_ref, cols_ref, order_ref, starts_ref = scalars
    tile = tiles_ref.shape[1]

    def step(p, carry):
        t = order_ref[p]
        at = pl.ds(pl.multiple_of((rows_ref[t] - row0) * tile, tile), tile)
        to = pl.ds(pl.multiple_of((cols_ref[t] - col0) * tile, tile), tile)
        out_ref[at, to] += tiles_ref[t].astype(F32)
        return carry

    lax.fori_loop(starts_ref[block], starts_ref[block + 1], step, 0)


def panel_kernel(rows_ref, cols_ref, order_ref, starts_ref, front_ref, tiles_ref, out_ref):
    out_ref[...] = front_ref[...]
    i = pl.program_id(0)
    high = out_ref.shape[0] // tiles_ref.shape[1]
    add_tiles((rows_ref, cols_ref, order_ref, starts_ref), tiles_ref, out_ref, i, i * high, 0)


def panel(place_rows, place_cols, front, tiles):
    rows = front.shape[0]
    tile = tiles.shape[1]
    high = min(rows, 512)
    steps = rows // high
    order, starts = bucket(place_rows, place_cols, high // tile, PW // tile, steps, 1)
    return pl.pallas_call(
        panel_kernel,
        out_shape=jax.ShapeDtypeStruct((rows, PW), F32),
        grid_spec=pltpu.PrefetchScalarGridSpec(
            num_scalar_prefetch=4,
            grid=(steps,),
            in_specs=[
                pl.BlockSpec((high, PW), lambda i, *_: (i, 0)),
                pl.BlockSpec(tiles.shape, lambda i, *_: (0, 0, 0), pipeline_mode=pl.Buffered(1)),
            ],
            out_specs=pl.BlockSpec((high, PW), lambda i, *_: (i, 0)),
        ),
        compiler_params=params(),
        name="panel",
    )(place_rows, place_cols, order, starts, front, tiles)


def spread(x, s):
    return jnp.broadcast_to(x[s : s + 1, :], x.shape)


def factor_block(sym):
    groups = BLK // 8
    rows = [sym[8 * v : 8 * v + 8, :] for v in range(groups)]
    lane = lax.broadcasted_iota(jnp.int32, (8, BLK), 1)
    sub = lax.broadcasted_iota(jnp.int32, (8, BLK), 0)
    for v0 in range(groups):
        first = 8 * v0
        cur = rows[v0]
        cols = [jnp.broadcast_to(cur[:, first + k : first + k + 1], (8, BLK)) for k in range(8)]
        scaled, mults = [], []
        for jj in range(8):
            at = lane == first + jj
            below = sub > jj
            inv = 1.0 / spread(cols[jj], jj)
            rs = jnp.where(at, inv, spread(cur, jj) * inv)
            mult = [None if k <= jj else spread(cols[k], jj) * inv for k in range(8)]
            f = jnp.where(below, cols[jj], 0.0)
            cur = jnp.where(at & below, 0.0, cur) - f * rs
            for k in range(jj + 1, 8):
                cols[k] = cols[k] - f * mult[k]
            scaled.append(jnp.where((lane > first + jj) & (lane < first + 8), 0.0, rs))
            mults.append(mult)
        rows[v0] = cur
        inside = (lane >= first) & (lane < first + 8)
        for v in range(v0 + 1, groups):
            cols = [
                jnp.broadcast_to(rows[v][:, first + k : first + k + 1], (8, BLK))
                for k in range(8)
            ]
            new = jnp.where(inside, 0.0, rows[v])
            for jj in range(8):
                new = new - cols[jj] * scaled[jj]
                for k in range(jj + 1, 8):
                    cols[k] = cols[k] - cols[jj] * mults[jj][k]
            rows[v] = new
    return jnp.concatenate(rows, axis=0)


def inverse_block(sym):
    done = factor_block(sym)
    row = lax.broadcasted_iota(jnp.int32, (BLK, BLK), 0)
    col = lax.broadcasted_iota(jnp.int32, (BLK, BLK), 1)
    diag = jnp.sum(jnp.where(row == col, done, 0.0), axis=1, keepdims=True)
    unit = jnp.where(row > col, done, jnp.where(row == col, 1.0, 0.0))
    return unit * lax.rsqrt(diag)


def first_kernel(rows_ref, cols_ref, front_ref, *refs, sources):
    tiles, (l_ref, trail_ref, pivot, work) = refs[:sources], refs[sources:]
    pivot[...] = front_ref[...]
    tile = tiles[0].shape[1]
    side = PW // tile
    for r, tile_ref in enumerate(tiles):
        for s in range(CAP):
            row, col = rows_ref[r * CAP + s], cols_ref[r * CAP + s]

            @pl.when((row >= 0) & (row < side) & (col < side))
            def _(row=row, col=col, tile_ref=tile_ref, s=s):
                at = pl.ds(pl.multiple_of(row * tile, tile), tile)
                to = pl.ds(pl.multiple_of(col * tile, tile), tile)
                pivot[at, to] += tile_ref[s].astype(F32)

    for i in range(PW // KP):
        for j in range(i + 1):
            si, sj = pl.ds(i * KP, KP), pl.ds(j * KP, KP)
            work[si, sj] = (pivot[si, sj] + pivot[sj, si].T) * 0.5
    eliminate(l_ref, trail_ref, work)


def next_kernel(a_ref, l_ref, *rest):
    work = rest[-1]
    work[...] = a_ref[...]
    eliminate(l_ref, rest[0] if len(rest) == 2 else None, work)


def eliminate(l_ref, trail_ref, work):
    n = work.shape[0]

    def step(b, carry):
        r0 = pl.multiple_of(b * BLK, BLK)
        inv = inverse_block(work[pl.ds(r0, BLK), pl.ds(r0, BLK)])
        l_ref[pl.ds(r0, BLK), pl.ds(r0, BLK)] = inv

        @pl.when(b == 0)
        def _():
            l_ref[0:BLK, BLK:KP] = jnp.zeros((BLK, KP - BLK), F32)
            low = dot_t(work[BLK:n, 0:BLK], inv)
            l_ref[BLK:n, 0:BLK] = low
            work[BLK:n, BLK:KP] -= dot_t(low, low[0:BLK])

        @pl.when(b == 1)
        def _():
            side = jnp.dot(
                l_ref[BLK:KP, 0:BLK], l_ref[0:BLK, 0:BLK], precision=HI, preferred_element_type=F32
            )
            l_ref[BLK:KP, 0:BLK] = -jnp.dot(inv, side, precision=HI, preferred_element_type=F32)
            if n > KP:
                l_ref[KP:n, BLK:KP] = dot_t(work[KP:n, BLK:KP], inv)

        return carry

    lax.fori_loop(0, KP // BLK, step, 0)
    if trail_ref is not None:
        m = n - KP
        for j in range(m // KP):
            rows = slice(j * KP, m)
            cols = slice(j * KP, (j + 1) * KP)
            low = l_ref[KP + j * KP : n, :]
            trail_ref[rows, cols] = work[KP + j * KP : n, KP + j * KP : KP + (j + 1) * KP] - dot_t(
                low, low[0:KP]
            )


def whole(shape):
    return pl.BlockSpec(shape, lambda i, *_: (0,) * len(shape))


def chol_first(place_rows, place_cols, front, gathered):
    shapes = [jax.ShapeDtypeStruct((PW, KP), F32), jax.ShapeDtypeStruct((PW - KP, PW - KP), F32)]
    return pl.pallas_call(
        functools.partial(first_kernel, sources=len(gathered)),
        out_shape=shapes,
        grid_spec=pltpu.PrefetchScalarGridSpec(
            num_scalar_prefetch=2,
            grid=(1,),
            in_specs=[whole((PW, PW))] + [whole(g.shape) for g in gathered],
            out_specs=[whole(s.shape) for s in shapes],
            scratch_shapes=[pltpu.VMEM((PW, PW), F32)] * 2,
        ),
        compiler_params=params(),
        name="chol",
    )(place_rows, place_cols, front, *gathered)


def chol_next(a):
    n = a.shape[0]
    shapes = [jax.ShapeDtypeStruct((n, KP), F32)]
    if n > KP:
        shapes.append(jax.ShapeDtypeStruct((n - KP, n - KP), F32))
    return pl.pallas_call(
        next_kernel,
        out_shape=shapes,
        grid=(1,),
        in_specs=[whole((n, n))],
        out_specs=[whole(s.shape) for s in shapes],
        scratch_shapes=[pltpu.VMEM((n, n), F32)],
        compiler_params=params(),
        name="chol",
    )(a)


def eye(n):
    return lax.broadcasted_iota(jnp.int32, (n, n), 0) == lax.broadcasted_iota(jnp.int32, (n, n), 1)


def solve_kernel(p_ref, *refs, k):
    factors, lowers = refs[:k], refs[k : 2 * k + 1]
    f_ref, q_ref = refs[2 * k + 1 :]
    for g in range(q_ref.shape[0]):
        at = slice(g * GRP, (g + 1) * GRP)
        acc = p_ref[at, :]
        for j in range(k):
            acc = acc - dot_t(factors[j][at, :], lowers[j][(k - j) * KP : (k - j + 1) * KP, :])
        f = dot_t(acc, lowers[k][0:KP, :])
        f_ref[at, :] = f
        peak = jnp.maximum(jnp.max(jnp.abs(f), axis=1, keepdims=True), 1e-30)
        code = jnp.ceil(jnp.log2(peak) * CODE)
        q = jnp.clip(jnp.round(f * (jnp.exp2(code * (-1.0 / CODE)) * TOP)), -TOP, TOP)
        q_ref[g, 0:GRP, :] = q.astype(jnp.int32).astype(jnp.int16)
        codes = jnp.sum(jnp.where(eye(GRP), code, 0.0), axis=0, keepdims=True)
        codes = jnp.broadcast_to(codes, (EXT, GRP))
        q_ref[g, GRP : GRP + EXT, :] = codes.astype(jnp.int32).astype(jnp.int16)


def solve(panel_sum, factors, lowers):
    k = len(factors)
    rows = panel_sum.shape[0]
    high = min(rows, 4 * GRP)
    block = pl.BlockSpec((high, KP), lambda i: (i, 0))
    return pl.pallas_call(
        functools.partial(solve_kernel, k=k),
        out_shape=[
            jax.ShapeDtypeStruct((rows, KP), F32),
            jax.ShapeDtypeStruct((rows // GRP, GRP + EXT, KP), jnp.int16),
        ],
        grid=(rows // high,),
        in_specs=[pl.BlockSpec((high, KP), lambda i: (i, k))]
        + [block] * k
        + [pl.BlockSpec(low.shape, lambda i: (0, 0)) for low in lowers],
        out_specs=[block, pl.BlockSpec((high // GRP, GRP + EXT, KP), lambda i: (i, 0, 0))],
        compiler_params=params(),
        name="solve",
    )(panel_sum, *factors, *lowers)


def decode(q_ref, g):
    codes = q_ref[g, GRP : GRP + EXT, :].astype(jnp.int32).astype(F32)[0:1, :]
    code = jnp.sum(jnp.where(eye(GRP), codes, 0.0), axis=1, keepdims=True)
    scale = jnp.exp2(code * (1.0 / CODE)) * (1.0 / TOP)
    return q_ref[g, 0:GRP, :].astype(jnp.int32).astype(F32) * scale


def halves(x):
    high = x.astype(jnp.bfloat16)
    return high, (x - high.astype(F32)).astype(jnp.bfloat16)


def schur_kernel(rows_ref, cols_ref, order_ref, starts_ref, member_ref, front_ref, tiles_ref, *refs, count):
    own, mine, other = refs[:count], refs[count : 2 * count], refs[2 * count : 3 * count]
    f_ref, out_ref, fh_ref, fl_ref, sh_ref, sl_ref = refs[3 * count :]
    i, j = pl.program_id(0), pl.program_id(1)
    groups = mine[0].shape[0]
    tile = tiles_ref.shape[1]

    @pl.when((i == 0) & (j == 0))
    def _():
        def step(g, carry):
            for e, strip in enumerate((mine, other)):
                member = member_ref[0] if e == 0 else 1 - member_ref[0]
                at = pl.ds(pl.multiple_of((member * groups + g) * GRP, GRP), GRP)
                for k in range(count):
                    high, low = halves(decode(strip[k], g))
                    sh_ref[at, k * KP : (k + 1) * KP] = high
                    sl_ref[at, k * KP : (k + 1) * KP] = low
            return carry

        lax.fori_loop(0, groups, step, 0)

    @pl.when(j == 0)
    def _():
        def step(g, carry):
            at = pl.ds(pl.multiple_of(g * GRP, GRP), GRP)
            for k in range(count):
                f = decode(own[k], g)
                f_ref[at, k * KP : (k + 1) * KP] = f
                high, low = halves(f)
                fh_ref[at, k * KP : (k + 1) * KP] = high
                fl_ref[at, k * KP : (k + 1) * KP] = low
            return carry

        lax.fori_loop(0, own[0].shape[0], step, 0)

    high, wide = out_ref.shape
    at = pl.ds(pl.multiple_of(j * wide, wide), wide)
    fh, fl, sh, sl = fh_ref[...], fl_ref[...], sh_ref[at, :], sl_ref[at, :]
    out_ref[...] = front_ref[...] - (dot_t(fh, sh, None) + (dot_t(fh, sl, None) + dot_t(fl, sh, None)))
    block = i * pl.num_programs(1) + j
    scalars = (rows_ref, cols_ref, order_ref, starts_ref)
    add_tiles(scalars, tiles_ref, out_ref, block, i * (high // tile), j * (wide // tile))


def schur(place_rows, place_cols, member, front, tiles, own, mine, other):
    rows, cols = front.shape
    count = len(own)
    once = pl.Buffered(1)
    high, wide = min(rows, 1024), min(cols, 512)
    depth = count * KP
    tile = tiles.shape[1]
    order, starts = bucket(place_rows, place_cols, high // tile, wide // tile, rows // high, cols // wide)
    block = pl.BlockSpec((high, wide), lambda i, j, *_: (i, j))
    coded = pl.BlockSpec((high // GRP, GRP + EXT, KP), lambda i, j, *_: (i, 0, 0))
    strip = pl.BlockSpec(mine[0].shape, lambda i, j, *_: (0, 0, 0), pipeline_mode=once)
    return pl.pallas_call(
        functools.partial(schur_kernel, count=count),
        out_shape=[jax.ShapeDtypeStruct((rows, PW), F32), jax.ShapeDtypeStruct((rows, cols), F32)],
        grid_spec=pltpu.PrefetchScalarGridSpec(
            num_scalar_prefetch=5,
            grid=(rows // high, cols // wide),
            in_specs=[block, pl.BlockSpec(tiles.shape, lambda i, j, *_: (0, 0, 0), pipeline_mode=once)]
            + [coded] * count
            + [strip] * (2 * count),
            out_specs=[pl.BlockSpec((high, depth), lambda i, j, *_: (i, 0)), block],
            scratch_shapes=[pltpu.VMEM((high, depth), jnp.bfloat16)] * 2
            + [pltpu.VMEM((cols, depth), jnp.bfloat16)] * 2,
        ),
        compiler_params=params(),
        name="schur",
    )(place_rows, place_cols, order, starts, member, front, tiles, *own, *mine, *other)


def gray(n):
    return [i ^ (i >> 1) for i in range(n)]


def ring_pairs(row_count, col_count, hop):
    chips = row_count // 2
    order = gray(chips)
    pairs = []
    for col in range(col_count):
        at = order.index(col)
        for member in range(2):
            way = 1 if member == 0 else -1
            src = order[(at + way * (hop - 1)) % chips] * 2 + member
            dst = order[(at + way * hop) % chips] * 2 + member
            pairs.append((src * col_count + col, dst * col_count + col))
    return pairs


def body(front_init, child_tiles, child_dest):
    row_count = lax.axis_size("row")
    col_count = lax.axis_size("col")
    if row_count != 2 * col_count:
        raise ValueError("mesh shape")
    row_extent, col_extent = front_init.shape
    tile_width = child_tiles.shape[1]
    tile_grid = col_extent * col_count // tile_width
    row_tiles = row_extent // tile_width
    col_tiles = col_extent // tile_width
    tile_count = child_tiles.shape[0]
    row_index = lax.axis_index("row")
    col_index = lax.axis_index("col")

    tile_row = child_dest // tile_grid
    tile_col = child_dest % tile_grid
    owner_row = tile_row // row_tiles
    local_tile = (tile_row - owner_row * row_tiles) * col_tiles + (tile_col - col_index * col_tiles)
    positions = jnp.arange(tile_count)
    earlier = positions[None, :] < positions[:, None]
    same_owner = owner_row[:, None] == owner_row[None, :]
    send_rank = jnp.sum((same_owner & earlier).astype(jnp.int32), axis=1)
    send_slot = owner_row * CAP + send_rank
    slots = jnp.arange(row_count * CAP)
    hit = slots[:, None] == send_slot[None, :]
    index = jnp.sum(jnp.where(hit, positions[None, :], 0), axis=1).astype(jnp.int32)
    targets = jnp.sum(jnp.where(hit, local_tile[None, :] + 1, 0), axis=1).astype(jnp.int32) - 1
    places = lax.all_to_all(targets, "row", split_axis=0, concat_axis=0, tiled=True)
    place_rows = jnp.where(places < 0, -1, places // col_tiles)
    place_cols = places % col_tiles

    both = ("row", "col")
    chips = row_count // 2
    member = row_index % 2
    order = jnp.array(gray(chips))
    here = jnp.argmax(order == row_index // 2)
    there = jnp.argmax(order == col_index)
    distance = jnp.where(member == 0, here - there, there - here) % chips
    swap = [(r * col_count + c, (r ^ 1) * col_count + c) for r in range(row_count) for c in range(col_count)]

    first = pack(index[:CAP], child_tiles)
    gathered = [first]
    for r in range(1, row_count):
        gathered.append(lax.ppermute(first, both, [(r * col_count, 0)]))
    outgoing = pack(index, child_tiles)
    arrived = lax.all_to_all(outgoing, "row", split_axis=0, concat_axis=0, tiled=True)
    panel_sum = panel(place_rows, place_cols, front_init, arrived)

    own, mine, other, factors, lowers = [], [], [], [], []
    pivot = None
    for k in range(PW // KP):
        if k == 0:
            result = chol_first(place_rows, place_cols, front_init, gathered)
        else:
            result = chol_next(pivot)
        pivot = result[-1]
        held = [result[0]]
        for chip in range(1, chips):
            parent = above(chip)
            pair = (2 * parent * col_count, 2 * chip * col_count)
            held.append(lax.ppermute(held[parent], both, [pair]))
        even = pick(row_index // 2, held)
        odd = lax.ppermute(even, both, [(2 * c * col_count, (2 * c + 1) * col_count) for c in range(chips)])
        lowers.append(pick(member, [even, odd]))
        factor, coded = solve(panel_sum, factors, lowers)
        factors.append(factor)
        steps = [coded]
        for hop in range(col_count - 1):
            steps.append(lax.ppermute(steps[-1], "col", [(hop, hop + 1)]))
        own.append(pick(col_index, steps))
        steps = [own[-1]]
        for hop in range(1, chips):
            steps.append(lax.ppermute(steps[-1], both, ring_pairs(row_count, col_count, hop)))
        mine.append(pick(distance, steps))
        other.append(lax.ppermute(mine[-1], both, swap))

    panel_factor, schur_update = schur(
        place_rows, place_cols, member.reshape(1).astype(jnp.int32), front_init, arrived, own, mine, other
    )
    return (panel_factor, schur_update)


def above(chip):
    return chip - (1 << (chip.bit_length() - 1))


def solution(mesh):
    return jax.shard_map(
        body,
        mesh=mesh,
        in_specs=(P("row", "col"), P(("row", "col"), None, None), P(("row", "col"))),
        out_specs=(P("row", None), P("row", "col")),
        check_vma=False,
    )
```

```python
import functools

import jax
import jax.numpy as jnp
from jax import lax
from jax.experimental import pallas as pl
from jax.experimental.pallas import tpu as pltpu
from jax.sharding import PartitionSpec as P


PW = 1024
CAP = 4
BLK = 128
KP = 256
GRP = 256
EXT = 16
CODE = 64.0
TOP = 32767.0
HI = lax.Precision.HIGHEST
F32 = jnp.float32
ANY = pl.BlockSpec(memory_space=pl.ANY)
VMEM_CAP = 58 << 20


def params(limit=VMEM_CAP):
    return pltpu.CompilerParams(vmem_limit_bytes=limit)


def dot_t(a, b, precision=HI):
    return lax.dot_general(
        a, b, (((1,), (1,)), ((), ())), precision=precision, preferred_element_type=F32
    )


def pack_kernel(idx_ref, src_ref, out_ref, held, sem_in, sem_out):
    slots = out_ref.shape[0]

    def fetch(s):
        return pltpu.make_async_copy(src_ref.at[idx_ref[s]], held.at[s], sem_in.at[s])

    def flush(s):
        return pltpu.make_async_copy(held.at[s], out_ref.at[s], sem_out.at[s])

    for s in range(slots):
        fetch(s).start()
    for s in range(slots):
        fetch(s).wait()
        flush(s).start()
    for s in range(slots):
        flush(s).wait()


def pack(index, tiles):
    slots = index.shape[0]
    shape = (slots,) + tiles.shape[1:]
    return pl.pallas_call(
        pack_kernel,
        out_shape=jax.ShapeDtypeStruct(shape, tiles.dtype),
        grid_spec=pltpu.PrefetchScalarGridSpec(
            num_scalar_prefetch=1,
            grid=(1,),
            in_specs=[ANY],
            out_specs=ANY,
            scratch_shapes=[
                pltpu.VMEM(shape, tiles.dtype),
                pltpu.SemaphoreType.DMA((slots,)),
                pltpu.SemaphoreType.DMA((slots,)),
            ],
        ),
        compiler_params=params(),
        name="pack",
    )(index, tiles)


PARTS = 4


def pick_kernel(idx_ref, *refs):
    sources, (out_ref, held, sem_in, sem_out) = refs[:-4], refs[-4:]
    step = out_ref.shape[0] // PARTS
    for i, source in enumerate(sources):

        @pl.when(idx_ref[0] == i)
        def _(source=source):
            for p in range(PARTS):
                at = pl.ds(p * step, step)
                pltpu.make_async_copy(source.at[at], held.at[at], sem_in.at[p]).start()

    flushes = []
    for p in range(PARTS):
        at = pl.ds(p * step, step)
        pltpu.make_async_copy(sources[0].at[at], held.at[at], sem_in.at[p]).wait()
        flush = pltpu.make_async_copy(held.at[at], out_ref.at[at], sem_out.at[p])
        flush.start()
        flushes.append(flush)
    for flush in flushes:
        flush.wait()


def pick(which, arrays):
    shape, dtype = arrays[0].shape, arrays[0].dtype
    return pl.pallas_call(
        pick_kernel,
        out_shape=jax.ShapeDtypeStruct(shape, dtype),
        grid_spec=pltpu.PrefetchScalarGridSpec(
            num_scalar_prefetch=1,
            grid=(1,),
            in_specs=[ANY] * len(arrays),
            out_specs=ANY,
            scratch_shapes=[
                pltpu.VMEM(shape, dtype),
                pltpu.SemaphoreType.DMA((PARTS,)),
                pltpu.SemaphoreType.DMA((PARTS,)),
            ],
        ),
        compiler_params=params(),
        name="pick",
    )(which.reshape(1).astype(jnp.int32), *arrays)


def bucket(rows, cols, high, wide, row_blocks, col_blocks):
    count = rows.shape[0]
    inside = (rows >= 0) & (cols < wide * col_blocks)
    key = jnp.where(inside, (rows // high) * col_blocks + cols // wide, row_blocks * col_blocks)
    at = jnp.arange(count)
    before = (key[None, :] < key[:, None]) | ((key[None, :] == key[:, None]) & (at[None, :] < at[:, None]))
    place = jnp.sum(before.astype(jnp.int32), axis=1)
    order = jnp.sum(jnp.where(place[None, :] == at[:, None], at[None, :], 0), axis=1).astype(jnp.int32)
    edges = jnp.arange(row_blocks * col_blocks + 1)
    starts = jnp.sum((key[None, :] < edges[:, None]).astype(jnp.int32), axis=1)
    return order, starts


def add_tiles(scalars, tiles_ref, out_ref, block, row0, col0):
    rows_ref, cols_ref, order_ref, starts_ref = scalars
    tile = tiles_ref.shape[1]

    def step(p, carry):
        t = order_ref[p]
        at = pl.ds(pl.multiple_of((rows_ref[t] - row0) * tile, tile), tile)
        to = pl.ds(pl.multiple_of((cols_ref[t] - col0) * tile, tile), tile)
        out_ref[at, to] += tiles_ref[t].astype(F32)
        return carry

    lax.fori_loop(starts_ref[block], starts_ref[block + 1], step, 0)


def panel_kernel(rows_ref, cols_ref, order_ref, starts_ref, front_ref, tiles_ref, out_ref):
    out_ref[...] = front_ref[...]
    i = pl.program_id(0)
    high = out_ref.shape[0] // tiles_ref.shape[1]
    add_tiles((rows_ref, cols_ref, order_ref, starts_ref), tiles_ref, out_ref, i, i * high, 0)


def panel(place_rows, place_cols, front, tiles):
    rows = front.shape[0]
    tile = tiles.shape[1]
    high = min(rows, 512)
    steps = rows // high
    order, starts = bucket(place_rows, place_cols, high // tile, PW // tile, steps, 1)
    return pl.pallas_call(
        panel_kernel,
        out_shape=jax.ShapeDtypeStruct((rows, PW), F32),
        grid_spec=pltpu.PrefetchScalarGridSpec(
            num_scalar_prefetch=4,
            grid=(steps,),
            in_specs=[
                pl.BlockSpec((high, PW), lambda i, *_: (i, 0)),
                pl.BlockSpec(tiles.shape, lambda i, *_: (0, 0, 0), pipeline_mode=pl.Buffered(1)),
            ],
            out_specs=pl.BlockSpec((high, PW), lambda i, *_: (i, 0)),
        ),
        compiler_params=params(),
        name="panel",
    )(place_rows, place_cols, order, starts, front, tiles)


def spread(x, s):
    return jnp.broadcast_to(x[s : s + 1, :], x.shape)


def factor_block(sym):
    groups = BLK // 8
    rows = [sym[8 * v : 8 * v + 8, :] for v in range(groups)]
    lane = lax.broadcasted_iota(jnp.int32, (8, BLK), 1)
    sub = lax.broadcasted_iota(jnp.int32, (8, BLK), 0)
    for v0 in range(groups):
        first = 8 * v0
        cur = rows[v0]
        cols = [jnp.broadcast_to(cur[:, first + k : first + k + 1], (8, BLK)) for k in range(8)]
        scaled, mults = [], []
        for jj in range(8):
            at = lane == first + jj
            below = sub > jj
            inv = 1.0 / spread(cols[jj], jj)
            rs = jnp.where(at, inv, spread(cur, jj) * inv)
            mult = [None if k <= jj else spread(cols[k], jj) * inv for k in range(8)]
            f = jnp.where(below, cols[jj], 0.0)
            cur = jnp.where(at & below, 0.0, cur) - f * rs
            for k in range(jj + 1, 8):
                cols[k] = cols[k] - f * mult[k]
            scaled.append(jnp.where((lane > first + jj) & (lane < first + 8), 0.0, rs))
            mults.append(mult)
        rows[v0] = cur
        inside = (lane >= first) & (lane < first + 8)
        for v in range(v0 + 1, groups):
            cols = [
                jnp.broadcast_to(rows[v][:, first + k : first + k + 1], (8, BLK))
                for k in range(8)
            ]
            new = jnp.where(inside, 0.0, rows[v])
            for jj in range(8):
                new = new - cols[jj] * scaled[jj]
                for k in range(jj + 1, 8):
                    cols[k] = cols[k] - cols[jj] * mults[jj][k]
            rows[v] = new
    return jnp.concatenate(rows, axis=0)


def inverse_block(sym):
    done = factor_block(sym)
    row = lax.broadcasted_iota(jnp.int32, (BLK, BLK), 0)
    col = lax.broadcasted_iota(jnp.int32, (BLK, BLK), 1)
    diag = jnp.sum(jnp.where(row == col, done, 0.0), axis=1, keepdims=True)
    unit = jnp.where(row > col, done, jnp.where(row == col, 1.0, 0.0))
    return unit * lax.rsqrt(diag)


def first_kernel(rows_ref, cols_ref, front_ref, tiles_ref, l_ref, trail_ref, pivot, work):
    pivot[...] = front_ref[...]
    slots, tile = tiles_ref.shape[:2]
    side = PW // tile

    def add(t, carry):
        row, col = rows_ref[t], cols_ref[t]

        @pl.when((row >= 0) & (row < side) & (col < side))
        def _():
            at = pl.ds(pl.multiple_of(row * tile, tile), tile)
            to = pl.ds(pl.multiple_of(col * tile, tile), tile)
            pivot[at, to] += tiles_ref[t].astype(F32)

        return carry

    lax.fori_loop(0, slots, add, 0)
    for i in range(PW // KP):
        for j in range(i + 1):
            si, sj = pl.ds(i * KP, KP), pl.ds(j * KP, KP)
            work[si, sj] = (pivot[si, sj] + pivot[sj, si].T) * 0.5
    eliminate(l_ref, trail_ref, work)


def next_kernel(a_ref, l_ref, *rest):
    work = rest[-1]
    work[...] = a_ref[...]
    eliminate(l_ref, rest[0] if len(rest) == 2 else None, work)


def eliminate(l_ref, trail_ref, work):
    n = work.shape[0]

    def step(b, carry):
        r0 = pl.multiple_of(b * BLK, BLK)
        inv = inverse_block(work[pl.ds(r0, BLK), pl.ds(r0, BLK)])
        l_ref[pl.ds(r0, BLK), pl.ds(r0, BLK)] = inv

        @pl.when(b == 0)
        def _():
            l_ref[0:BLK, BLK:KP] = jnp.zeros((BLK, KP - BLK), F32)
            low = dot_t(work[BLK:n, 0:BLK], inv)
            l_ref[BLK:n, 0:BLK] = low
            work[BLK:n, BLK:KP] -= dot_t(low, low[0:BLK])

        @pl.when(b == 1)
        def _():
            side = jnp.dot(
                l_ref[BLK:KP, 0:BLK], l_ref[0:BLK, 0:BLK], precision=HI, preferred_element_type=F32
            )
            l_ref[BLK:KP, 0:BLK] = -jnp.dot(inv, side, precision=HI, preferred_element_type=F32)
            if n > KP:
                l_ref[KP:n, BLK:KP] = dot_t(work[KP:n, BLK:KP], inv)

        return carry

    lax.fori_loop(0, KP // BLK, step, 0)
    if trail_ref is not None:
        m = n - KP
        for j in range(m // KP):
            rows = slice(j * KP, m)
            cols = slice(j * KP, (j + 1) * KP)
            low = l_ref[KP + j * KP : n, :]
            trail_ref[rows, cols] = work[KP + j * KP : n, KP + j * KP : KP + (j + 1) * KP] - dot_t(
                low, low[0:KP]
            )


def whole(shape):
    return pl.BlockSpec(shape, lambda i, *_: (0,) * len(shape))


def chol_first(place_rows, place_cols, front, tiles):
    shapes = [jax.ShapeDtypeStruct((PW, KP), F32), jax.ShapeDtypeStruct((PW - KP, PW - KP), F32)]
    return pl.pallas_call(
        first_kernel,
        out_shape=shapes,
        grid_spec=pltpu.PrefetchScalarGridSpec(
            num_scalar_prefetch=2,
            grid=(1,),
            in_specs=[whole((PW, PW)), whole(tiles.shape)],
            out_specs=[whole(s.shape) for s in shapes],
            scratch_shapes=[pltpu.VMEM((PW, PW), F32)] * 2,
        ),
        compiler_params=params(),
        name="chol",
    )(place_rows, place_cols, front, tiles)


def chol_next(a):
    n = a.shape[0]
    shapes = [jax.ShapeDtypeStruct((n, KP), F32)]
    if n > KP:
        shapes.append(jax.ShapeDtypeStruct((n - KP, n - KP), F32))
    return pl.pallas_call(
        next_kernel,
        out_shape=shapes,
        grid=(1,),
        in_specs=[whole((n, n))],
        out_specs=[whole(s.shape) for s in shapes],
        scratch_shapes=[pltpu.VMEM((n, n), F32)],
        compiler_params=params(),
        name="chol",
    )(a)


def eye(n):
    return lax.broadcasted_iota(jnp.int32, (n, n), 0) == lax.broadcasted_iota(jnp.int32, (n, n), 1)


def halves(x):
    high = x.astype(jnp.bfloat16)
    return high, (x - high.astype(F32)).astype(jnp.bfloat16)


def dot_halves(a, b):
    return dot_t(a[0], b[0], None) + (dot_t(a[0], b[1], None) + dot_t(a[1], b[0], None))


def solve_kernel(row_ref, p_ref, *refs, k, sources):
    factors, lowers, held = refs[:k], refs[k : 2 * k], refs[2 * k : 2 * k + sources]
    f_ref, q_ref, low_ref, sem = refs[2 * k + sources :]

    @pl.when(pl.program_id(0) == 0)
    def _():
        for r, source in enumerate(held):

            @pl.when(row_ref[0] == r)
            def _(source=source):
                copy = pltpu.make_async_copy(source, low_ref, sem)
                copy.start()
                copy.wait()

    sides = [halves(lowers[j][(k - j) * KP : (k - j + 1) * KP, :]) for j in range(k)]
    top = halves(low_ref[0:KP, :])
    for g in range(q_ref.shape[0]):
        at = slice(g * GRP, (g + 1) * GRP)
        acc = p_ref[at, :]
        for j in range(k):
            acc = acc - dot_halves(halves(factors[j][at, :]), sides[j])
        f = dot_halves(halves(acc), top)
        f_ref[at, :] = f
        peak = jnp.maximum(jnp.max(jnp.abs(f), axis=1, keepdims=True), 1e-30)
        code = jnp.ceil(jnp.log2(peak) * CODE)
        q = jnp.clip(jnp.round(f * (jnp.exp2(code * (-1.0 / CODE)) * TOP)), -TOP, TOP)
        q_ref[g, 0:GRP, :] = q.astype(jnp.int32).astype(jnp.int16)
        codes = jnp.sum(jnp.where(eye(GRP), code, 0.0), axis=0, keepdims=True)
        codes = jnp.broadcast_to(codes, (EXT, GRP))
        q_ref[g, GRP : GRP + EXT, :] = codes.astype(jnp.int32).astype(jnp.int16)


def solve(row, panel_sum, factors, lowers, held):
    k = len(factors)
    rows = panel_sum.shape[0]
    high = min(rows, 4 * GRP)
    block = pl.BlockSpec((high, KP), lambda i, *_: (i, 0))
    return pl.pallas_call(
        functools.partial(solve_kernel, k=k, sources=len(held)),
        out_shape=[
            jax.ShapeDtypeStruct((rows, KP), F32),
            jax.ShapeDtypeStruct((rows // GRP, GRP + EXT, KP), jnp.int16),
            jax.ShapeDtypeStruct(held[0].shape, F32),
        ],
        grid_spec=pltpu.PrefetchScalarGridSpec(
            num_scalar_prefetch=1,
            grid=(rows // high,),
            in_specs=[pl.BlockSpec((high, KP), lambda i, *_: (i, k))]
            + [block] * k
            + [whole(low.shape) for low in lowers]
            + [ANY] * len(held),
            out_specs=[
                block,
                pl.BlockSpec((high // GRP, GRP + EXT, KP), lambda i, *_: (i, 0, 0)),
                whole(held[0].shape),
            ],
            scratch_shapes=[pltpu.SemaphoreType.DMA],
        ),
        compiler_params=params(),
        name="solve",
    )(row, panel_sum, *factors, *lowers, *held)


def decode(q_ref, g):
    codes = q_ref[g, GRP : GRP + EXT, :].astype(jnp.int32).astype(F32)[0:1, :]
    code = jnp.sum(jnp.where(eye(GRP), codes, 0.0), axis=1, keepdims=True)
    scale = jnp.exp2(code * (1.0 / CODE)) * (1.0 / TOP)
    return q_ref[g, 0:GRP, :].astype(jnp.int32).astype(F32) * scale


PIECES = 4


def stash(f, k, at, high_ref, low_ref):
    high, low = halves(f)
    high_ref[at, k * KP : (k + 1) * KP] = high
    low_ref[at, k * KP : (k + 1) * KP] = low


def piece_kernel(
    rows_ref, cols_ref, order_ref, starts_ref, member_ref, front_ref, tiles_ref, *refs, piece, count
):
    own, mine, other = refs[:count], refs[count : 2 * count], refs[2 * count : 3 * count]
    sh_ref, sl_ref = refs[-2:]
    outs = refs[3 * count + (piece > 0) : -2]
    out_ref = outs[0]
    i = pl.program_id(0)
    groups = mine[0].shape[0]
    tile = tiles_ref.shape[1]

    @pl.when(i == 0)
    def _():
        for e, strip in enumerate((mine, other)):

            @pl.when(member_ref[0] == (e + (2 * piece) // PIECES) % 2)
            def _(strip=strip):
                def step(g, carry):
                    at = pl.ds(pl.multiple_of(g * GRP, GRP), GRP)
                    for k in range(count):
                        stash(decode(strip[k], g), k, at, sh_ref, sl_ref)
                    return carry

                lax.fori_loop(0, groups, step, 0)

    high, wide = out_ref.shape
    for g in range(high // GRP):
        at = slice(g * GRP, (g + 1) * GRP)
        f = jnp.concatenate([decode(own[k], g) for k in range(count)], axis=1)
        if piece == 0:
            outs[1][at, :] = f
        prod = dot_halves(halves(f), (sh_ref[...], sl_ref[...]))
        out_ref[at, :] = front_ref[at, :] - prod
    scalars = (rows_ref, cols_ref, order_ref, starts_ref)
    block = i * PIECES + piece
    add_tiles(scalars, tiles_ref, out_ref, block, i * (high // tile), piece * (wide // tile))


def schur_piece(piece, scalars, member, front, tiles, own, mine, other, previous):
    rows, cols = front.shape
    count = len(own)
    high, wide = min(rows, 512), cols // PIECES
    depth = count * KP
    block = pl.BlockSpec((high, wide), lambda i, *_: (i, piece))
    coded = pl.BlockSpec((high // GRP, GRP + EXT, KP), lambda i, *_: (i, 0, 0))
    strip = pl.BlockSpec(
        (wide // GRP, GRP + EXT, KP), lambda i, *_: (piece % (PIECES // 2), 0, 0), pipeline_mode=pl.Buffered(1)
    )
    shapes, specs = [jax.ShapeDtypeStruct((rows, cols), F32)], [block]
    if piece == 0:
        shapes.append(jax.ShapeDtypeStruct((rows, PW), F32))
        specs.append(pl.BlockSpec((high, depth), lambda i, *_: (i, 0)))
    return pl.pallas_call(
        functools.partial(piece_kernel, piece=piece, count=count),
        out_shape=shapes,
        grid_spec=pltpu.PrefetchScalarGridSpec(
            num_scalar_prefetch=5,
            grid=(rows // high,),
            in_specs=[
                block,
                pl.BlockSpec(tiles.shape, lambda i, *_: (0, 0, 0), pipeline_mode=pl.Buffered(1)),
            ]
            + [coded] * count
            + [strip] * (2 * count)
            + [ANY] * len(previous),
            out_specs=specs,
            scratch_shapes=[pltpu.VMEM((wide, depth), jnp.bfloat16)] * 2,
        ),
        input_output_aliases={7 + 3 * count: 0} if previous else {},
        compiler_params=params(),
        name="piece",
    )(*scalars, member, front, tiles, *own, *mine, *other, *previous)


def schur_kernel(member_ref, front_ref, *refs, count):
    own, mine, other = refs[:count], refs[count : 2 * count], refs[2 * count : 3 * count]
    out_ref, f_ref, fh_ref, fl_ref, sh_ref, sl_ref = refs[3 * count + 1 :]
    i, j = pl.program_id(0), pl.program_id(1)
    groups = mine[0].shape[0]

    @pl.when((i == 0) & (j == 0))
    def _():
        def step(g, carry):
            for e, strip in enumerate((mine, other)):
                member = member_ref[0] if e == 0 else 1 - member_ref[0]
                at = pl.ds(pl.multiple_of((member * groups + g) * GRP, GRP), GRP)
                for k in range(count):
                    stash(decode(strip[k], g), k, at, sh_ref, sl_ref)
            return carry

        lax.fori_loop(0, groups, step, 0)

    @pl.when(j == 0)
    def _():
        def step(g, carry):
            at = pl.ds(pl.multiple_of(g * GRP, GRP), GRP)
            for k in range(count):
                f = decode(own[k], g)
                f_ref[at, k * KP : (k + 1) * KP] = f
                stash(f, k, at, fh_ref, fl_ref)
            return carry

        lax.fori_loop(0, own[0].shape[0], step, 0)

    wide = out_ref.shape[1]
    at = pl.ds(pl.multiple_of(j * wide, wide), wide)
    prod = dot_halves((fh_ref[...], fl_ref[...]), (sh_ref[at, :], sl_ref[at, :]))
    out_ref[...] = front_ref[...] - prod


def schur_rest(member, front, factor, own, mine, other):
    rows, cols = front.shape
    count = len(own)
    high, wide = min(rows, 1024), min(cols, 1024)
    depth = count * KP
    block = pl.BlockSpec((high, wide), lambda i, j, *_: (i, j))
    coded = pl.BlockSpec((high // GRP, GRP + EXT, KP), lambda i, j, *_: (i, 0, 0))
    strip = pl.BlockSpec(mine[0].shape, lambda i, j, *_: (0, 0, 0), pipeline_mode=pl.Buffered(1))
    return pl.pallas_call(
        functools.partial(schur_kernel, count=count),
        out_shape=[jax.ShapeDtypeStruct((rows, cols), F32), jax.ShapeDtypeStruct((rows, PW), F32)],
        grid_spec=pltpu.PrefetchScalarGridSpec(
            num_scalar_prefetch=1,
            grid=(rows // high, cols // wide),
            in_specs=[block] + [coded] * count + [strip] * (2 * count) + [ANY],
            out_specs=[block, pl.BlockSpec((high, depth), lambda i, j, *_: (i, PW // depth - 1))],
            scratch_shapes=[pltpu.VMEM((high, depth), jnp.bfloat16)] * 2
            + [pltpu.VMEM((cols, depth), jnp.bfloat16)] * 2,
        ),
        input_output_aliases={1: 0, 2 + 3 * count: 1},
        compiler_params=params(),
        name="schur",
    )(member, front, *own, *mine, *other, factor)


def gray(n):
    return [i ^ (i >> 1) for i in range(n)]


def ring_pairs(row_count, col_count, hop):
    chips = row_count // 2
    order = gray(chips)
    pairs = []
    for col in range(col_count):
        at = order.index(col)
        for member in range(2):
            way = 1 if member == 0 else -1
            src = order[(at + way * (hop - 1)) % chips] * 2 + member
            dst = order[(at + way * hop) % chips] * 2 + member
            pairs.append((src * col_count + col, dst * col_count + col))
    return pairs


def body(front_init, child_tiles, child_dest):
    row_count = lax.axis_size("row")
    col_count = lax.axis_size("col")
    if row_count != 2 * col_count:
        raise ValueError("mesh shape")
    row_extent, col_extent = front_init.shape
    tile_width = child_tiles.shape[1]
    tile_grid = col_extent * col_count // tile_width
    row_tiles = row_extent // tile_width
    col_tiles = col_extent // tile_width
    tile_count = child_tiles.shape[0]
    row_index = lax.axis_index("row")
    col_index = lax.axis_index("col")

    tile_row = child_dest // tile_grid
    tile_col = child_dest % tile_grid
    owner_row = tile_row // row_tiles
    local_tile = (tile_row - owner_row * row_tiles) * col_tiles + (tile_col - col_index * col_tiles)
    positions = jnp.arange(tile_count)
    earlier = positions[None, :] < positions[:, None]
    same_owner = owner_row[:, None] == owner_row[None, :]
    send_rank = jnp.sum((same_owner & earlier).astype(jnp.int32), axis=1)
    send_slot = owner_row * CAP + send_rank
    slots = jnp.arange(row_count * CAP)
    hit = slots[:, None] == send_slot[None, :]
    index = jnp.sum(jnp.where(hit, positions[None, :], 0), axis=1).astype(jnp.int32)
    targets = jnp.sum(jnp.where(hit, local_tile[None, :] + 1, 0), axis=1).astype(jnp.int32) - 1
    places = lax.all_to_all(targets, "row", split_axis=0, concat_axis=0, tiled=True)
    place_rows = jnp.where(places < 0, -1, places // col_tiles)
    place_cols = places % col_tiles

    both = ("row", "col")
    chips = row_count // 2
    member = row_index % 2
    order = jnp.array(gray(chips))
    here = jnp.argmax(order == row_index // 2)
    there = jnp.argmax(order == col_index)
    distance = jnp.where(member == 0, here - there, there - here) % chips
    swap = [(r * col_count + c, (r ^ 1) * col_count + c) for r in range(row_count) for c in range(col_count)]

    outgoing = pack(index, child_tiles)
    arrived = lax.all_to_all(outgoing, "row", split_axis=0, concat_axis=0, tiled=True)

    count = PW // KP
    row = row_index.reshape(1).astype(jnp.int32)
    own, mine, other, factors, lowers = [], [], [], [], []
    result = chol_first(place_rows, place_cols, front_init, arrived)
    panel_sum = panel(place_rows, place_cols, front_init, arrived)
    for k in range(count):
        if k > 0:
            result = chol_next(result[-1])
        even = [result[0]]
        for chip in range(1, chips):
            parent = above(chip)
            pair = (2 * parent * col_count, 2 * chip * col_count)
            even.append(lax.ppermute(even[parent], both, [pair]))
        held = []
        for chip in range(chips):
            pair = (2 * chip * col_count, (2 * chip + 1) * col_count)
            held += [even[chip], lax.ppermute(even[chip], both, [pair])]
        factor, coded, lower = solve(row, panel_sum, factors, lowers, held)
        factors.append(factor)
        lowers.append(lower)
        steps = [coded]
        for hop in range(col_count - 1):
            steps.append(lax.ppermute(steps[-1], "col", [(hop, hop + 1)]))
        own.append(pick(col_index, steps))
        steps = [own[-1]]
        for hop in range(1, chips):
            steps.append(lax.ppermute(steps[-1], both, ring_pairs(row_count, col_count, hop)))
        mine.append(pick(distance, steps))
        other.append(lax.ppermute(mine[-1], both, swap))

    member = member.reshape(1).astype(jnp.int32)
    part = count // 2
    high = min(row_extent, 512)
    scalars = (place_rows, place_cols) + bucket(
        place_rows,
        place_cols,
        high // tile_width,
        col_tiles // PIECES,
        row_extent // high,
        PIECES,
    )
    previous, factor = [], None
    for piece in range(PIECES):
        result = schur_piece(
            piece,
            scalars,
            member,
            front_init,
            arrived,
            own[:part],
            mine[:part],
            other[:part],
            previous,
        )
        previous = [result[0]]
        if piece == 0:
            factor = result[1]
    schur_update, panel_factor = schur_rest(
        member, previous[0], factor, own[part:], mine[part:], other[part:]
    )
    return (panel_factor, schur_update)


def above(chip):
    return chip - (1 << (chip.bit_length() - 1))


def solution(mesh):
    return jax.shard_map(
        body,
        mesh=mesh,
        in_specs=(P("row", "col"), P(("row", "col"), None, None), P(("row", "col"))),
        out_specs=(P("row", None), P("row", "col")),
        check_vma=False,
    )
```

```python
import functools

import jax
import jax.numpy as jnp
from jax import lax
from jax.experimental import pallas as pl
from jax.experimental.pallas import tpu as pltpu
from jax.sharding import PartitionSpec as P


PW = 1024
CAP = 4
BLK = 128
KP = 256
GRP = 256
EXT = 16
CODE = 64.0
TOP = 32767.0
HI = lax.Precision.HIGHEST
F32 = jnp.float32
ANY = pl.BlockSpec(memory_space=pl.ANY)
VMEM_CAP = 58 << 20


def params(limit=VMEM_CAP):
    return pltpu.CompilerParams(vmem_limit_bytes=limit)


def dot_t(a, b, precision=HI):
    return lax.dot_general(
        a, b, (((1,), (1,)), ((), ())), precision=precision, preferred_element_type=F32
    )


def pack_kernel(idx_ref, src_ref, out_ref, held, sem_in, sem_out):
    slots = out_ref.shape[0]

    def fetch(s):
        return pltpu.make_async_copy(src_ref.at[idx_ref[s]], held.at[s], sem_in.at[s])

    def flush(s):
        return pltpu.make_async_copy(held.at[s], out_ref.at[s], sem_out.at[s])

    for s in range(slots):
        fetch(s).start()
    for s in range(slots):
        fetch(s).wait()
        flush(s).start()
    for s in range(slots):
        flush(s).wait()


def pack(index, tiles):
    slots = index.shape[0]
    shape = (slots,) + tiles.shape[1:]
    return pl.pallas_call(
        pack_kernel,
        out_shape=jax.ShapeDtypeStruct(shape, tiles.dtype),
        grid_spec=pltpu.PrefetchScalarGridSpec(
            num_scalar_prefetch=1,
            grid=(1,),
            in_specs=[ANY],
            out_specs=ANY,
            scratch_shapes=[
                pltpu.VMEM(shape, tiles.dtype),
                pltpu.SemaphoreType.DMA((slots,)),
                pltpu.SemaphoreType.DMA((slots,)),
            ],
        ),
        compiler_params=params(),
        name="pack",
    )(index, tiles)


PARTS = 4


def pick_kernel(idx_ref, *refs):
    sources, (out_ref, held, sem_in, sem_out) = refs[:-4], refs[-4:]
    step = out_ref.shape[0] // PARTS
    for i, source in enumerate(sources):

        @pl.when(idx_ref[0] == i)
        def _(source=source):
            for p in range(PARTS):
                at = pl.ds(p * step, step)
                pltpu.make_async_copy(source.at[at], held.at[at], sem_in.at[p]).start()

    flushes = []
    for p in range(PARTS):
        at = pl.ds(p * step, step)
        pltpu.make_async_copy(sources[0].at[at], held.at[at], sem_in.at[p]).wait()
        flush = pltpu.make_async_copy(held.at[at], out_ref.at[at], sem_out.at[p])
        flush.start()
        flushes.append(flush)
    for flush in flushes:
        flush.wait()


def pick(which, arrays):
    shape, dtype = arrays[0].shape, arrays[0].dtype
    return pl.pallas_call(
        pick_kernel,
        out_shape=jax.ShapeDtypeStruct(shape, dtype),
        grid_spec=pltpu.PrefetchScalarGridSpec(
            num_scalar_prefetch=1,
            grid=(1,),
            in_specs=[ANY] * len(arrays),
            out_specs=ANY,
            scratch_shapes=[
                pltpu.VMEM(shape, dtype),
                pltpu.SemaphoreType.DMA((PARTS,)),
                pltpu.SemaphoreType.DMA((PARTS,)),
            ],
        ),
        compiler_params=params(),
        name="pick",
    )(which.reshape(1).astype(jnp.int32), *arrays)


def bucket(rows, cols, high, wide, row_blocks, col_blocks):
    count = rows.shape[0]
    inside = (rows >= 0) & (cols < wide * col_blocks)
    key = jnp.where(inside, (rows // high) * col_blocks + cols // wide, row_blocks * col_blocks)
    at = jnp.arange(count)
    before = (key[None, :] < key[:, None]) | ((key[None, :] == key[:, None]) & (at[None, :] < at[:, None]))
    place = jnp.sum(before.astype(jnp.int32), axis=1)
    order = jnp.sum(jnp.where(place[None, :] == at[:, None], at[None, :], 0), axis=1).astype(jnp.int32)
    edges = jnp.arange(row_blocks * col_blocks + 1)
    starts = jnp.sum((key[None, :] < edges[:, None]).astype(jnp.int32), axis=1)
    return order, starts


def add_tiles(scalars, tiles_ref, out_ref, block, row0, col0):
    rows_ref, cols_ref, order_ref, starts_ref = scalars
    tile = tiles_ref.shape[1]

    def step(p, carry):
        t = order_ref[p]
        at = pl.ds(pl.multiple_of((rows_ref[t] - row0) * tile, tile), tile)
        to = pl.ds(pl.multiple_of((cols_ref[t] - col0) * tile, tile), tile)
        out_ref[at, to] += tiles_ref[t].astype(F32)
        return carry

    lax.fori_loop(starts_ref[block], starts_ref[block + 1], step, 0)


def panel_kernel(active_ref, rows_ref, cols_ref, order_ref, starts_ref, front_ref, tiles_ref, out_ref):
    @pl.when(active_ref[0] == 1)
    def _():
        out_ref[...] = front_ref[...]
        i = pl.program_id(0)
        high = out_ref.shape[0] // tiles_ref.shape[1]
        add_tiles((rows_ref, cols_ref, order_ref, starts_ref), tiles_ref, out_ref, i, i * high, 0)


def panel(active, place_rows, place_cols, front, tiles):
    rows = front.shape[0]
    tile = tiles.shape[1]
    high = min(rows, 512)
    steps = rows // high
    order, starts = bucket(place_rows, place_cols, high // tile, PW // tile, steps, 1)
    return pl.pallas_call(
        panel_kernel,
        out_shape=jax.ShapeDtypeStruct((rows, PW), F32),
        grid_spec=pltpu.PrefetchScalarGridSpec(
            num_scalar_prefetch=5,
            grid=(steps,),
            in_specs=[
                pl.BlockSpec((high, PW), lambda i, active, *_: (i * active[0], 0)),
                pl.BlockSpec(tiles.shape, lambda i, *_: (0, 0, 0), pipeline_mode=pl.Buffered(1)),
            ],
            out_specs=pl.BlockSpec((high, PW), lambda i, active, *_: (i * active[0], 0)),
        ),
        compiler_params=params(),
        name="panel",
    )(active, place_rows, place_cols, order, starts, front, tiles)


def spread(x, s):
    return jnp.broadcast_to(x[s : s + 1, :], x.shape)


def factor_block(sym):
    groups = BLK // 8
    rows = [sym[8 * v : 8 * v + 8, :] for v in range(groups)]
    lane = lax.broadcasted_iota(jnp.int32, (8, BLK), 1)
    sub = lax.broadcasted_iota(jnp.int32, (8, BLK), 0)
    for v0 in range(groups):
        first = 8 * v0
        cur = rows[v0]
        cols = [jnp.broadcast_to(cur[:, first + k : first + k + 1], (8, BLK)) for k in range(8)]
        scaled, mults = [], []
        for jj in range(8):
            at = lane == first + jj
            below = sub > jj
            inv = 1.0 / spread(cols[jj], jj)
            rs = jnp.where(at, inv, spread(cur, jj) * inv)
            mult = [None if k <= jj else spread(cols[k], jj) * inv for k in range(8)]
            f = jnp.where(below, cols[jj], 0.0)
            cur = jnp.where(at & below, 0.0, cur) - f * rs
            for k in range(jj + 1, 8):
                cols[k] = cols[k] - f * mult[k]
            scaled.append(jnp.where((lane > first + jj) & (lane < first + 8), 0.0, rs))
            mults.append(mult)
        rows[v0] = cur
        inside = (lane >= first) & (lane < first + 8)
        for v in range(v0 + 1, groups):
            cols = [
                jnp.broadcast_to(rows[v][:, first + k : first + k + 1], (8, BLK))
                for k in range(8)
            ]
            new = jnp.where(inside, 0.0, rows[v])
            for jj in range(8):
                new = new - cols[jj] * scaled[jj]
                for k in range(jj + 1, 8):
                    cols[k] = cols[k] - cols[jj] * mults[jj][k]
            rows[v] = new
    return jnp.concatenate(rows, axis=0)


def inverse_block(sym):
    done = factor_block(sym)
    row = lax.broadcasted_iota(jnp.int32, (BLK, BLK), 0)
    col = lax.broadcasted_iota(jnp.int32, (BLK, BLK), 1)
    diag = jnp.sum(jnp.where(row == col, done, 0.0), axis=1, keepdims=True)
    unit = jnp.where(row > col, done, jnp.where(row == col, 1.0, 0.0))
    return unit * lax.rsqrt(diag)


def first_kernel(active_ref, rows_ref, cols_ref, front_ref, tiles_ref, l_ref, trail_ref, pivot, work):
    @pl.when(active_ref[0] == 1)
    def _():
        first_step(rows_ref, cols_ref, front_ref, tiles_ref, l_ref, trail_ref, pivot, work)


def first_step(rows_ref, cols_ref, front_ref, tiles_ref, l_ref, trail_ref, pivot, work):
    pivot[...] = front_ref[...]
    slots, tile = tiles_ref.shape[:2]
    side = PW // tile

    def add(t, carry):
        row, col = rows_ref[t], cols_ref[t]

        @pl.when((row >= 0) & (row < side) & (col < side))
        def _():
            at = pl.ds(pl.multiple_of(row * tile, tile), tile)
            to = pl.ds(pl.multiple_of(col * tile, tile), tile)
            pivot[at, to] += tiles_ref[t].astype(F32)

        return carry

    lax.fori_loop(0, slots, add, 0)
    for i in range(PW // KP):
        for j in range(i + 1):
            si, sj = pl.ds(i * KP, KP), pl.ds(j * KP, KP)
            work[si, sj] = (pivot[si, sj] + pivot[sj, si].T) * 0.5
    eliminate(l_ref, trail_ref, work)


def next_kernel(active_ref, a_ref, l_ref, *rest):
    @pl.when(active_ref[0] == 1)
    def _():
        work = rest[-1]
        work[...] = a_ref[...]
        eliminate(l_ref, rest[0] if len(rest) == 2 else None, work)


def eliminate(l_ref, trail_ref, work):
    n = work.shape[0]

    def step(b, carry):
        r0 = pl.multiple_of(b * BLK, BLK)
        inv = inverse_block(work[pl.ds(r0, BLK), pl.ds(r0, BLK)])
        l_ref[pl.ds(r0, BLK), pl.ds(r0, BLK)] = inv

        @pl.when(b == 0)
        def _():
            l_ref[0:BLK, BLK:KP] = jnp.zeros((BLK, KP - BLK), F32)
            low = dot_t(work[BLK:n, 0:BLK], inv)
            l_ref[BLK:n, 0:BLK] = low
            work[BLK:n, BLK:KP] -= dot_t(low, low[0:BLK])

        @pl.when(b == 1)
        def _():
            side = jnp.dot(
                l_ref[BLK:KP, 0:BLK], l_ref[0:BLK, 0:BLK], precision=HI, preferred_element_type=F32
            )
            l_ref[BLK:KP, 0:BLK] = -jnp.dot(inv, side, precision=HI, preferred_element_type=F32)
            if n > KP:
                l_ref[KP:n, BLK:KP] = dot_t(work[KP:n, BLK:KP], inv)

        return carry

    lax.fori_loop(0, KP // BLK, step, 0)
    if trail_ref is not None:
        m = n - KP
        for j in range(m // KP):
            rows = slice(j * KP, m)
            cols = slice(j * KP, (j + 1) * KP)
            low = l_ref[KP + j * KP : n, :]
            trail_ref[rows, cols] = work[KP + j * KP : n, KP + j * KP : KP + (j + 1) * KP] - dot_t(
                low, low[0:KP]
            )


def whole(shape):
    return pl.BlockSpec(shape, lambda i, *_: (0,) * len(shape))


def chol_first(active, place_rows, place_cols, front, tiles):
    shapes = [jax.ShapeDtypeStruct((PW, KP), F32), jax.ShapeDtypeStruct((PW - KP, PW - KP), F32)]
    return pl.pallas_call(
        first_kernel,
        out_shape=shapes,
        grid_spec=pltpu.PrefetchScalarGridSpec(
            num_scalar_prefetch=3,
            grid=(1,),
            in_specs=[whole((PW, PW)), whole(tiles.shape)],
            out_specs=[whole(s.shape) for s in shapes],
            scratch_shapes=[pltpu.VMEM((PW, PW), F32)] * 2,
        ),
        compiler_params=params(),
        name="chol",
    )(active, place_rows, place_cols, front, tiles)


def chol_next(active, a):
    n = a.shape[0]
    shapes = [jax.ShapeDtypeStruct((n, KP), F32)]
    if n > KP:
        shapes.append(jax.ShapeDtypeStruct((n - KP, n - KP), F32))
    return pl.pallas_call(
        next_kernel,
        out_shape=shapes,
        grid_spec=pltpu.PrefetchScalarGridSpec(
            num_scalar_prefetch=1,
            grid=(1,),
            in_specs=[whole((n, n))],
            out_specs=[whole(s.shape) for s in shapes],
            scratch_shapes=[pltpu.VMEM((n, n), F32)],
        ),
        compiler_params=params(),
        name="chol",
    )(active, a)


def eye(n):
    return lax.broadcasted_iota(jnp.int32, (n, n), 0) == lax.broadcasted_iota(jnp.int32, (n, n), 1)


def halves(x):
    high = x.astype(jnp.bfloat16)
    return high, (x - high.astype(F32)).astype(jnp.bfloat16)


def dot_halves(a, b):
    return dot_t(a[0], b[0], None) + (dot_t(a[0], b[1], None) + dot_t(a[1], b[0], None))


def solve_kernel(row_ref, p_ref, *refs, k, sources):
    @pl.when(row_ref[1] == 1)
    def _():
        solve_step(row_ref, p_ref, *refs, k=k, sources=sources)


def solve_step(row_ref, p_ref, *refs, k, sources):
    factors, lowers, held = refs[:k], refs[k : 2 * k], refs[2 * k : 2 * k + sources]
    f_ref, q_ref, low_ref, sem = refs[2 * k + sources :]

    @pl.when(pl.program_id(0) == 0)
    def _():
        for r, source in enumerate(held):

            @pl.when(row_ref[0] == r)
            def _(source=source):
                copy = pltpu.make_async_copy(source, low_ref, sem)
                copy.start()
                copy.wait()

    sides = [halves(lowers[j][(k - j) * KP : (k - j + 1) * KP, :]) for j in range(k)]
    top = halves(low_ref[0:KP, :])
    for g in range(q_ref.shape[0]):
        at = slice(g * GRP, (g + 1) * GRP)
        acc = p_ref[at, :]
        for j in range(k):
            acc = acc - dot_halves(halves(factors[j][at, :]), sides[j])
        f = dot_halves(halves(acc), top)
        f_ref[at, :] = f
        peak = jnp.maximum(jnp.max(jnp.abs(f), axis=1, keepdims=True), 1e-30)
        code = jnp.ceil(jnp.log2(peak) * CODE)
        q = jnp.clip(jnp.round(f * (jnp.exp2(code * (-1.0 / CODE)) * TOP)), -TOP, TOP)
        q_ref[g, 0:GRP, :] = q.astype(jnp.int32).astype(jnp.int16)
        codes = jnp.sum(jnp.where(eye(GRP), code, 0.0), axis=0, keepdims=True)
        codes = jnp.broadcast_to(codes, (EXT, GRP))
        q_ref[g, GRP : GRP + EXT, :] = codes.astype(jnp.int32).astype(jnp.int16)


def solve(row, panel_sum, factors, lowers, held):
    k = len(factors)
    rows = panel_sum.shape[0]
    high = min(rows, 4 * GRP)
    block = pl.BlockSpec((high, KP), lambda i, row: (i * row[1], 0))
    return pl.pallas_call(
        functools.partial(solve_kernel, k=k, sources=len(held)),
        out_shape=[
            jax.ShapeDtypeStruct((rows, KP), F32),
            jax.ShapeDtypeStruct((rows // GRP, GRP + EXT, KP), jnp.int16),
            jax.ShapeDtypeStruct(held[0].shape, F32),
        ],
        grid_spec=pltpu.PrefetchScalarGridSpec(
            num_scalar_prefetch=1,
            grid=(rows // high,),
            in_specs=[pl.BlockSpec((high, KP), lambda i, row: (i * row[1], k))]
            + [block] * k
            + [whole(low.shape) for low in lowers]
            + [ANY] * len(held),
            out_specs=[
                block,
                pl.BlockSpec((high // GRP, GRP + EXT, KP), lambda i, row: (i * row[1], 0, 0)),
                whole(held[0].shape),
            ],
            scratch_shapes=[pltpu.SemaphoreType.DMA],
        ),
        compiler_params=params(),
        name="solve",
    )(row, panel_sum, *factors, *lowers, *held)


def decode(q_ref, g):
    codes = q_ref[g, GRP : GRP + EXT, :].astype(jnp.int32).astype(F32)[0:1, :]
    code = jnp.sum(jnp.where(eye(GRP), codes, 0.0), axis=1, keepdims=True)
    scale = jnp.exp2(code * (1.0 / CODE)) * (1.0 / TOP)
    return q_ref[g, 0:GRP, :].astype(jnp.int32).astype(F32) * scale


PIECES = 4


def stash(f, k, at, high_ref, low_ref):
    high, low = halves(f)
    high_ref[at, k * KP : (k + 1) * KP] = high
    low_ref[at, k * KP : (k + 1) * KP] = low


def piece_kernel(
    rows_ref, cols_ref, order_ref, starts_ref, member_ref, front_ref, tiles_ref, *refs, piece, count
):
    own, mine, other = refs[:count], refs[count : 2 * count], refs[2 * count : 3 * count]
    sh_ref, sl_ref = refs[-2:]
    outs = refs[3 * count + (piece > 0) : -2]
    out_ref = outs[0]
    i = pl.program_id(0)
    groups = mine[0].shape[0]
    tile = tiles_ref.shape[1]

    @pl.when(i == 0)
    def _():
        for e, strip in enumerate((mine, other)):

            @pl.when(member_ref[0] == (e + (2 * piece) // PIECES) % 2)
            def _(strip=strip):
                def step(g, carry):
                    at = pl.ds(pl.multiple_of(g * GRP, GRP), GRP)
                    for k in range(count):
                        stash(decode(strip[k], g), k, at, sh_ref, sl_ref)
                    return carry

                lax.fori_loop(0, groups, step, 0)

    high, wide = out_ref.shape
    for g in range(high // GRP):
        at = slice(g * GRP, (g + 1) * GRP)
        f = jnp.concatenate([decode(own[k], g) for k in range(count)], axis=1)
        if piece == 0:
            outs[1][at, :] = f
        prod = dot_halves(halves(f), (sh_ref[...], sl_ref[...]))
        out_ref[at, :] = front_ref[at, :] - prod
    scalars = (rows_ref, cols_ref, order_ref, starts_ref)
    block = i * PIECES + piece
    add_tiles(scalars, tiles_ref, out_ref, block, i * (high // tile), piece * (wide // tile))


def schur_piece(piece, scalars, member, front, tiles, own, mine, other, previous):
    rows, cols = front.shape
    count = len(own)
    high, wide = min(rows, 512), cols // PIECES
    depth = count * KP
    block = pl.BlockSpec((high, wide), lambda i, *_: (i, piece))
    coded = pl.BlockSpec((high // GRP, GRP + EXT, KP), lambda i, *_: (i, 0, 0))
    strip = pl.BlockSpec(
        (wide // GRP, GRP + EXT, KP), lambda i, *_: (piece % (PIECES // 2), 0, 0), pipeline_mode=pl.Buffered(1)
    )
    shapes, specs = [jax.ShapeDtypeStruct((rows, cols), F32)], [block]
    if piece == 0:
        shapes.append(jax.ShapeDtypeStruct((rows, PW), F32))
        specs.append(pl.BlockSpec((high, depth), lambda i, *_: (i, 0)))
    return pl.pallas_call(
        functools.partial(piece_kernel, piece=piece, count=count),
        out_shape=shapes,
        grid_spec=pltpu.PrefetchScalarGridSpec(
            num_scalar_prefetch=5,
            grid=(rows // high,),
            in_specs=[
                block,
                pl.BlockSpec(tiles.shape, lambda i, *_: (0, 0, 0), pipeline_mode=pl.Buffered(1)),
            ]
            + [coded] * count
            + [strip] * (2 * count)
            + [ANY] * len(previous),
            out_specs=specs,
            scratch_shapes=[pltpu.VMEM((wide, depth), jnp.bfloat16)] * 2,
        ),
        input_output_aliases={7 + 3 * count: 0} if previous else {},
        compiler_params=params(),
        name="piece",
    )(*scalars, member, front, tiles, *own, *mine, *other, *previous)


def schur_kernel(member_ref, front_ref, *refs, count):
    own, mine, other = refs[:count], refs[count : 2 * count], refs[2 * count : 3 * count]
    out_ref, f_ref, fh_ref, fl_ref, sh_ref, sl_ref = refs[3 * count + 1 :]
    i, j = pl.program_id(0), pl.program_id(1)
    groups = mine[0].shape[0]

    @pl.when((i == 0) & (j == 0))
    def _():
        def step(g, carry):
            for e, strip in enumerate((mine, other)):
                member = member_ref[0] if e == 0 else 1 - member_ref[0]
                at = pl.ds(pl.multiple_of((member * groups + g) * GRP, GRP), GRP)
                for k in range(count):
                    stash(decode(strip[k], g), k, at, sh_ref, sl_ref)
            return carry

        lax.fori_loop(0, groups, step, 0)

    @pl.when(j == 0)
    def _():
        def step(g, carry):
            at = pl.ds(pl.multiple_of(g * GRP, GRP), GRP)
            for k in range(count):
                f = decode(own[k], g)
                f_ref[at, k * KP : (k + 1) * KP] = f
                stash(f, k, at, fh_ref, fl_ref)
            return carry

        lax.fori_loop(0, own[0].shape[0], step, 0)

    wide = out_ref.shape[1]
    at = pl.ds(pl.multiple_of(j * wide, wide), wide)
    prod = dot_halves((fh_ref[...], fl_ref[...]), (sh_ref[at, :], sl_ref[at, :]))
    out_ref[...] = front_ref[...] - prod


def schur_rest(member, front, factor, own, mine, other):
    rows, cols = front.shape
    count = len(own)
    high, wide = min(rows, 1024), min(cols, 1024)
    depth = count * KP
    block = pl.BlockSpec((high, wide), lambda i, j, *_: (i, j))
    coded = pl.BlockSpec((high // GRP, GRP + EXT, KP), lambda i, j, *_: (i, 0, 0))
    strip = pl.BlockSpec(mine[0].shape, lambda i, j, *_: (0, 0, 0), pipeline_mode=pl.Buffered(1))
    return pl.pallas_call(
        functools.partial(schur_kernel, count=count),
        out_shape=[jax.ShapeDtypeStruct((rows, cols), F32), jax.ShapeDtypeStruct((rows, PW), F32)],
        grid_spec=pltpu.PrefetchScalarGridSpec(
            num_scalar_prefetch=1,
            grid=(rows // high, cols // wide),
            in_specs=[block] + [coded] * count + [strip] * (2 * count) + [ANY],
            out_specs=[block, pl.BlockSpec((high, depth), lambda i, j, *_: (i, PW // depth - 1))],
            scratch_shapes=[pltpu.VMEM((high, depth), jnp.bfloat16)] * 2
            + [pltpu.VMEM((cols, depth), jnp.bfloat16)] * 2,
        ),
        input_output_aliases={1: 0, 2 + 3 * count: 1},
        compiler_params=params(),
        name="schur",
    )(member, front, *own, *mine, *other, factor)


def gray(n):
    return [i ^ (i >> 1) for i in range(n)]


def ring_pairs(row_count, col_count, hop, turn):
    chips = row_count // 2
    order = gray(chips)
    pairs = []
    for col in range(col_count):
        at = order.index(col)
        for member in range(2):
            way = turn if member == 0 else -turn
            src = order[(at + way * (hop - 1)) % chips] * 2 + member
            dst = order[(at + way * hop) % chips] * 2 + member
            pairs.append((src * col_count + col, dst * col_count + col))
    return pairs


def body(front_init, child_tiles, child_dest):
    row_count = lax.axis_size("row")
    col_count = lax.axis_size("col")
    if row_count != 2 * col_count:
        raise ValueError("mesh shape")
    row_extent, col_extent = front_init.shape
    tile_width = child_tiles.shape[1]
    tile_grid = col_extent * col_count // tile_width
    row_tiles = row_extent // tile_width
    col_tiles = col_extent // tile_width
    tile_count = child_tiles.shape[0]
    row_index = lax.axis_index("row")
    col_index = lax.axis_index("col")

    tile_row = child_dest // tile_grid
    tile_col = child_dest % tile_grid
    owner_row = tile_row // row_tiles
    local_tile = (tile_row - owner_row * row_tiles) * col_tiles + (tile_col - col_index * col_tiles)
    positions = jnp.arange(tile_count)
    earlier = positions[None, :] < positions[:, None]
    same_owner = owner_row[:, None] == owner_row[None, :]
    send_rank = jnp.sum((same_owner & earlier).astype(jnp.int32), axis=1)
    send_slot = owner_row * CAP + send_rank
    slots = jnp.arange(row_count * CAP)
    hit = slots[:, None] == send_slot[None, :]
    index = jnp.sum(jnp.where(hit, positions[None, :], 0), axis=1).astype(jnp.int32)
    targets = jnp.sum(jnp.where(hit, local_tile[None, :] + 1, 0), axis=1).astype(jnp.int32) - 1
    places = lax.all_to_all(targets, "row", split_axis=0, concat_axis=0, tiled=True)
    place_rows = jnp.where(places < 0, -1, places // col_tiles)
    place_cols = places % col_tiles

    both = ("row", "col")
    chips = row_count // 2
    member = row_index % 2
    order = jnp.array(gray(chips))
    here = jnp.argmax(order == row_index // 2)
    there = jnp.argmax(order == col_index)
    distance = jnp.where(member == 0, here - there, there - here) % chips
    swap = [(r * col_count + c, (r ^ 1) * col_count + c) for r in range(row_count) for c in range(col_count)]

    outgoing = pack(index, child_tiles)
    arrived = lax.all_to_all(outgoing, "row", split_axis=0, concat_axis=0, tiled=True)

    count = PW // KP
    at_first = (col_index == 0).astype(jnp.int32)
    row = jnp.stack([row_index.astype(jnp.int32), at_first])
    active = at_first.reshape(1)
    root = active * (row_index == 0).astype(jnp.int32)
    own, mine, other, factors, lowers = [], [], [], [], []
    result = chol_first(root, place_rows, place_cols, front_init, arrived)
    panel_sum = panel(active, place_rows, place_cols, front_init, arrived)
    for k in range(count):
        if k > 0:
            result = chol_next(root, result[-1])
        even = [result[0]]
        for chip in range(1, chips):
            parent = above(chip)
            pair = (2 * parent * col_count, 2 * chip * col_count)
            even.append(lax.ppermute(even[parent], both, [pair]))
        held = []
        for chip in range(chips):
            pair = (2 * chip * col_count, (2 * chip + 1) * col_count)
            held += [even[chip], lax.ppermute(even[chip], both, [pair])]
        factor, coded, lower = solve(row, panel_sum, factors, lowers, held)
        factors.append(factor)
        lowers.append(lower)
        steps = [coded]
        for hop in range(col_count - 1):
            steps.append(lax.ppermute(steps[-1], "col", [(hop, hop + 1)]))
        own.append(pick(col_index, steps))
        ahead, back = [own[-1]], [own[-1]]
        for hop in range(1, chips // 2 + 1):
            ahead.append(lax.ppermute(ahead[-1], both, ring_pairs(row_count, col_count, hop, 1)))
        for hop in range(1, chips - chips // 2):
            back.append(lax.ppermute(back[-1], both, ring_pairs(row_count, col_count, hop, -1)))
        mine.append(pick(distance, ahead + back[:0:-1]))
        other.append(lax.ppermute(mine[-1], both, swap))

    member = member.reshape(1).astype(jnp.int32)
    part = count // 2
    high = min(row_extent, 512)
    scalars = (place_rows, place_cols) + bucket(
        place_rows,
        place_cols,
        high // tile_width,
        col_tiles // PIECES,
        row_extent // high,
        PIECES,
    )
    previous, factor = [], None
    for piece in range(PIECES):
        result = schur_piece(
            piece,
            scalars,
            member,
            front_init,
            arrived,
            own[:part],
            mine[:part],
            other[:part],
            previous,
        )
        previous = [result[0]]
        if piece == 0:
            factor = result[1]
    schur_update, panel_factor = schur_rest(
        member, previous[0], factor, own[part:], mine[part:], other[part:]
    )
    return (panel_factor, schur_update)


def above(chip):
    return chip - (1 << (chip.bit_length() - 1))


def solution(mesh):
    return jax.shard_map(
        body,
        mesh=mesh,
        in_specs=(P("row", "col"), P(("row", "col"), None, None), P(("row", "col"))),
        out_specs=(P("row", None), P("row", "col")),
        check_vma=False,
    )
```

```python
import functools

import jax
import jax.numpy as jnp
from jax import lax
from jax.experimental import pallas as pl
from jax.experimental.pallas import tpu as pltpu
from jax.sharding import PartitionSpec as P


PW = 1024
CAP = 4
BLK = 128
KP = 256
GRP = 256
EXT = 16
CODE = 64.0
TOP = 32767.0
HI = lax.Precision.HIGHEST
F32 = jnp.float32
ANY = pl.BlockSpec(memory_space=pl.ANY)
VMEM_CAP = 58 << 20


def params(limit=VMEM_CAP):
    return pltpu.CompilerParams(vmem_limit_bytes=limit)


def dot_t(a, b, precision=HI):
    return lax.dot_general(
        a, b, (((1,), (1,)), ((), ())), precision=precision, preferred_element_type=F32
    )


def pack_kernel(idx_ref, src_ref, out_ref, held, sem_in, sem_out):
    slots = out_ref.shape[0]

    def fetch(s):
        return pltpu.make_async_copy(src_ref.at[idx_ref[s]], held.at[s], sem_in.at[s])

    def flush(s):
        return pltpu.make_async_copy(held.at[s], out_ref.at[s], sem_out.at[s])

    for s in range(slots):
        fetch(s).start()
    for s in range(slots):
        fetch(s).wait()
        flush(s).start()
    for s in range(slots):
        flush(s).wait()


def pack(index, tiles):
    slots = index.shape[0]
    shape = (slots,) + tiles.shape[1:]
    return pl.pallas_call(
        pack_kernel,
        out_shape=jax.ShapeDtypeStruct(shape, tiles.dtype),
        grid_spec=pltpu.PrefetchScalarGridSpec(
            num_scalar_prefetch=1,
            grid=(1,),
            in_specs=[ANY],
            out_specs=ANY,
            scratch_shapes=[
                pltpu.VMEM(shape, tiles.dtype),
                pltpu.SemaphoreType.DMA((slots,)),
                pltpu.SemaphoreType.DMA((slots,)),
            ],
        ),
        compiler_params=params(),
        name="pack",
    )(index, tiles)


PARTS = 4


def pick_kernel(idx_ref, *refs):
    sources, (out_ref, held, sem_in, sem_out) = refs[:-4], refs[-4:]
    step = out_ref.shape[0] // PARTS
    for i, source in enumerate(sources):

        @pl.when(idx_ref[0] == i)
        def _(source=source):
            for p in range(PARTS):
                at = pl.ds(p * step, step)
                pltpu.make_async_copy(source.at[at], held.at[at], sem_in.at[p]).start()

    flushes = []
    for p in range(PARTS):
        at = pl.ds(p * step, step)
        pltpu.make_async_copy(sources[0].at[at], held.at[at], sem_in.at[p]).wait()
        flush = pltpu.make_async_copy(held.at[at], out_ref.at[at], sem_out.at[p])
        flush.start()
        flushes.append(flush)
    for flush in flushes:
        flush.wait()


def pick(which, arrays):
    shape, dtype = arrays[0].shape, arrays[0].dtype
    return pl.pallas_call(
        pick_kernel,
        out_shape=jax.ShapeDtypeStruct(shape, dtype),
        grid_spec=pltpu.PrefetchScalarGridSpec(
            num_scalar_prefetch=1,
            grid=(1,),
            in_specs=[ANY] * len(arrays),
            out_specs=ANY,
            scratch_shapes=[
                pltpu.VMEM(shape, dtype),
                pltpu.SemaphoreType.DMA((PARTS,)),
                pltpu.SemaphoreType.DMA((PARTS,)),
            ],
        ),
        compiler_params=params(),
        name="pick",
    )(which.reshape(1).astype(jnp.int32), *arrays)


def bucket(rows, cols, high, wide, row_blocks, col_blocks):
    count = rows.shape[0]
    inside = (rows >= 0) & (cols < wide * col_blocks)
    key = jnp.where(inside, (rows // high) * col_blocks + cols // wide, row_blocks * col_blocks)
    at = jnp.arange(count)
    before = (key[None, :] < key[:, None]) | ((key[None, :] == key[:, None]) & (at[None, :] < at[:, None]))
    place = jnp.sum(before.astype(jnp.int32), axis=1)
    order = jnp.sum(jnp.where(place[None, :] == at[:, None], at[None, :], 0), axis=1).astype(jnp.int32)
    edges = jnp.arange(row_blocks * col_blocks + 1)
    starts = jnp.sum((key[None, :] < edges[:, None]).astype(jnp.int32), axis=1)
    return order, starts


def add_tiles(scalars, tiles_ref, out_ref, block, row0, col0):
    rows_ref, cols_ref, order_ref, starts_ref = scalars
    tile = tiles_ref.shape[1]

    def step(p, carry):
        t = order_ref[p]
        at = pl.ds(pl.multiple_of((rows_ref[t] - row0) * tile, tile), tile)
        to = pl.ds(pl.multiple_of((cols_ref[t] - col0) * tile, tile), tile)
        out_ref[at, to] += tiles_ref[t].astype(F32)
        return carry

    lax.fori_loop(starts_ref[block], starts_ref[block + 1], step, 0)


def panel_kernel(active_ref, rows_ref, cols_ref, order_ref, starts_ref, front_ref, tiles_ref, out_ref):
    @pl.when(active_ref[0] == 1)
    def _():
        out_ref[...] = front_ref[...]
        i = pl.program_id(0)
        high = out_ref.shape[0] // tiles_ref.shape[1]
        add_tiles((rows_ref, cols_ref, order_ref, starts_ref), tiles_ref, out_ref, i, i * high, 0)


def panel(active, place_rows, place_cols, front, tiles):
    rows = front.shape[0]
    tile = tiles.shape[1]
    high = min(rows, 512)
    steps = rows // high
    order, starts = bucket(place_rows, place_cols, high // tile, PW // tile, steps, 1)
    return pl.pallas_call(
        panel_kernel,
        out_shape=jax.ShapeDtypeStruct((rows, PW), F32),
        grid_spec=pltpu.PrefetchScalarGridSpec(
            num_scalar_prefetch=5,
            grid=(steps,),
            in_specs=[
                pl.BlockSpec((high, PW), lambda i, active, *_: (i * active[0], 0)),
                pl.BlockSpec(tiles.shape, lambda i, *_: (0, 0, 0), pipeline_mode=pl.Buffered(1)),
            ],
            out_specs=pl.BlockSpec((high, PW), lambda i, active, *_: (i * active[0], 0)),
        ),
        compiler_params=params(),
        name="panel",
    )(active, place_rows, place_cols, order, starts, front, tiles)


def spread(x, s):
    return jnp.broadcast_to(x[s : s + 1, :], x.shape)


def factor_block(sym):
    groups = BLK // 8
    rows = [sym[8 * v : 8 * v + 8, :] for v in range(groups)]
    lane = lax.broadcasted_iota(jnp.int32, (8, BLK), 1)
    sub = lax.broadcasted_iota(jnp.int32, (8, BLK), 0)
    for v0 in range(groups):
        first = 8 * v0
        cur = rows[v0]
        cols = [jnp.broadcast_to(cur[:, first + k : first + k + 1], (8, BLK)) for k in range(8)]
        scaled, mults = [], []
        for jj in range(8):
            at = lane == first + jj
            below = sub > jj
            inv = 1.0 / spread(cols[jj], jj)
            rs = jnp.where(at, inv, spread(cur, jj) * inv)
            mult = [None if k <= jj else spread(cols[k], jj) * inv for k in range(8)]
            f = jnp.where(below, cols[jj], 0.0)
            cur = jnp.where(at & below, 0.0, cur) - f * rs
            for k in range(jj + 1, 8):
                cols[k] = cols[k] - f * mult[k]
            scaled.append(jnp.where((lane > first + jj) & (lane < first + 8), 0.0, rs))
            mults.append(mult)
        rows[v0] = cur
        inside = (lane >= first) & (lane < first + 8)
        for v in range(v0 + 1, groups):
            cols = [
                jnp.broadcast_to(rows[v][:, first + k : first + k + 1], (8, BLK))
                for k in range(8)
            ]
            new = jnp.where(inside, 0.0, rows[v])
            for jj in range(8):
                new = new - cols[jj] * scaled[jj]
                for k in range(jj + 1, 8):
                    cols[k] = cols[k] - cols[jj] * mults[jj][k]
            rows[v] = new
    return jnp.concatenate(rows, axis=0)


def inverse_block(sym):
    done = factor_block(sym)
    row = lax.broadcasted_iota(jnp.int32, (BLK, BLK), 0)
    col = lax.broadcasted_iota(jnp.int32, (BLK, BLK), 1)
    diag = jnp.sum(jnp.where(row == col, done, 0.0), axis=1, keepdims=True)
    unit = jnp.where(row > col, done, jnp.where(row == col, 1.0, 0.0))
    return unit * lax.rsqrt(diag)


def first_kernel(active_ref, rows_ref, cols_ref, front_ref, tiles_ref, l_ref, trail_ref, pivot, work):
    @pl.when(active_ref[0] == 1)
    def _():
        first_step(rows_ref, cols_ref, front_ref, tiles_ref, l_ref, trail_ref, pivot, work)


def first_step(rows_ref, cols_ref, front_ref, tiles_ref, l_ref, trail_ref, pivot, work):
    pivot[...] = front_ref[...]
    slots, tile = tiles_ref.shape[:2]
    side = PW // tile

    def add(t, carry):
        row, col = rows_ref[t], cols_ref[t]

        @pl.when((row >= 0) & (row < side) & (col < side))
        def _():
            at = pl.ds(pl.multiple_of(row * tile, tile), tile)
            to = pl.ds(pl.multiple_of(col * tile, tile), tile)
            pivot[at, to] += tiles_ref[t].astype(F32)

        return carry

    lax.fori_loop(0, slots, add, 0)
    for i in range(PW // KP):
        for j in range(i + 1):
            si, sj = pl.ds(i * KP, KP), pl.ds(j * KP, KP)
            work[si, sj] = (pivot[si, sj] + pivot[sj, si].T) * 0.5
    eliminate(l_ref, trail_ref, work)


def rest_kernel(active_ref, a_ref, l_ref, *works):
    @pl.when(active_ref[0] == 1)
    def _():
        works[0][...] = a_ref[...]
        start = 0
        for work, after in zip(works, works[1:] + (None,)):
            n = work.shape[0]
            eliminate(l_ref.at[pl.ds(start, n)], after, work)
            start += n


def eliminate(l_ref, trail_ref, work):
    n = work.shape[0]

    def step(b, carry):
        r0 = pl.multiple_of(b * BLK, BLK)
        inv = inverse_block(work[pl.ds(r0, BLK), pl.ds(r0, BLK)])
        l_ref[pl.ds(r0, BLK), pl.ds(r0, BLK)] = inv

        @pl.when(b == 0)
        def _():
            l_ref[0:BLK, BLK:KP] = jnp.zeros((BLK, KP - BLK), F32)
            low = dot_t(work[BLK:n, 0:BLK], inv)
            l_ref[BLK:n, 0:BLK] = low
            work[BLK:n, BLK:KP] -= dot_t(low, low[0:BLK])

        @pl.when(b == 1)
        def _():
            side = jnp.dot(
                l_ref[BLK:KP, 0:BLK], l_ref[0:BLK, 0:BLK], precision=HI, preferred_element_type=F32
            )
            l_ref[BLK:KP, 0:BLK] = -jnp.dot(inv, side, precision=HI, preferred_element_type=F32)
            if n > KP:
                l_ref[KP:n, BLK:KP] = dot_t(work[KP:n, BLK:KP], inv)

        return carry

    lax.fori_loop(0, KP // BLK, step, 0)
    if trail_ref is not None:
        m = n - KP
        for j in range(m // KP):
            rows = slice(j * KP, m)
            cols = slice(j * KP, (j + 1) * KP)
            low = l_ref[KP + j * KP : n, :]
            trail_ref[rows, cols] = work[KP + j * KP : n, KP + j * KP : KP + (j + 1) * KP] - dot_t(
                low, low[0:KP]
            )


def whole(shape):
    return pl.BlockSpec(shape, lambda i, *_: (0,) * len(shape))


def chol_first(active, place_rows, place_cols, front, tiles):
    shapes = [jax.ShapeDtypeStruct((PW, KP), F32), jax.ShapeDtypeStruct((PW - KP, PW - KP), F32)]
    return pl.pallas_call(
        first_kernel,
        out_shape=shapes,
        grid_spec=pltpu.PrefetchScalarGridSpec(
            num_scalar_prefetch=3,
            grid=(1,),
            in_specs=[whole((PW, PW)), whole(tiles.shape)],
            out_specs=[whole(s.shape) for s in shapes],
            scratch_shapes=[pltpu.VMEM((PW, PW), F32)] * 2,
        ),
        compiler_params=params(),
        name="chol",
    )(active, place_rows, place_cols, front, tiles)


def chol_rest(active, a):
    sides = range(a.shape[0], 0, -KP)
    out = jax.ShapeDtypeStruct((sum(sides), KP), F32)
    return pl.pallas_call(
        rest_kernel,
        out_shape=out,
        grid_spec=pltpu.PrefetchScalarGridSpec(
            num_scalar_prefetch=1,
            grid=(1,),
            in_specs=[whole(a.shape)],
            out_specs=whole(out.shape),
            scratch_shapes=[pltpu.VMEM((n, n), F32) for n in sides],
        ),
        compiler_params=params(),
        name="chol",
    )(active, a)


def eye(n):
    return lax.broadcasted_iota(jnp.int32, (n, n), 0) == lax.broadcasted_iota(jnp.int32, (n, n), 1)


def halves(x):
    high = x.astype(jnp.bfloat16)
    return high, (x - high.astype(F32)).astype(jnp.bfloat16)


def dot_halves(a, b):
    return dot_t(a[0], b[0], None) + (dot_t(a[0], b[1], None) + dot_t(a[1], b[0], None))


def solve_kernel(row_ref, p_ref, *refs, k, sources, start):
    @pl.when(row_ref[1] == 1)
    def _():
        solve_step(row_ref, p_ref, *refs, k=k, sources=sources, start=start)


def solve_step(row_ref, p_ref, *refs, k, sources, start):
    factors, lowers, held = refs[:k], refs[k : 2 * k], refs[2 * k : 2 * k + sources]
    f_ref, q_ref, low_ref, sem = refs[2 * k + sources :]

    @pl.when(pl.program_id(0) == 0)
    def _():
        for r, source in enumerate(held):

            @pl.when(row_ref[0] == r)
            def _(source=source):
                copy = pltpu.make_async_copy(source.at[pl.ds(start, low_ref.shape[0])], low_ref, sem)
                copy.start()
                copy.wait()

    sides = [halves(lowers[j][(k - j) * KP : (k - j + 1) * KP, :]) for j in range(k)]
    top = halves(low_ref[0:KP, :])
    for g in range(q_ref.shape[0]):
        at = slice(g * GRP, (g + 1) * GRP)
        acc = p_ref[at, :]
        for j in range(k):
            acc = acc - dot_halves(halves(factors[j][at, :]), sides[j])
        f = dot_halves(halves(acc), top)
        f_ref[at, :] = f
        peak = jnp.maximum(jnp.max(jnp.abs(f), axis=1, keepdims=True), 1e-30)
        code = jnp.ceil(jnp.log2(peak) * CODE)
        q = jnp.clip(jnp.round(f * (jnp.exp2(code * (-1.0 / CODE)) * TOP)), -TOP, TOP)
        q_ref[g, 0:GRP, :] = q.astype(jnp.int32).astype(jnp.int16)
        codes = jnp.sum(jnp.where(eye(GRP), code, 0.0), axis=0, keepdims=True)
        codes = jnp.broadcast_to(codes, (EXT, GRP))
        q_ref[g, GRP : GRP + EXT, :] = codes.astype(jnp.int32).astype(jnp.int16)


def solve(row, panel_sum, factors, lowers, held):
    k = len(factors)
    low = (PW - k * KP, KP)
    start = sum(range(PW - KP, low[0], -KP))
    rows = panel_sum.shape[0]
    high = min(rows, 4 * GRP)
    block = pl.BlockSpec((high, KP), lambda i, row: (i * row[1], 0))
    return pl.pallas_call(
        functools.partial(solve_kernel, k=k, sources=len(held), start=start),
        out_shape=[
            jax.ShapeDtypeStruct((rows, KP), F32),
            jax.ShapeDtypeStruct((rows // GRP, GRP + EXT, KP), jnp.int16),
            jax.ShapeDtypeStruct(low, F32),
        ],
        grid_spec=pltpu.PrefetchScalarGridSpec(
            num_scalar_prefetch=1,
            grid=(rows // high,),
            in_specs=[pl.BlockSpec((high, KP), lambda i, row: (i * row[1], k))]
            + [block] * k
            + [whole(low.shape) for low in lowers]
            + [ANY] * len(held),
            out_specs=[
                block,
                pl.BlockSpec((high // GRP, GRP + EXT, KP), lambda i, row: (i * row[1], 0, 0)),
                whole(low),
            ],
            scratch_shapes=[pltpu.SemaphoreType.DMA],
        ),
        compiler_params=params(),
        name="solve",
    )(row, panel_sum, *factors, *lowers, *held)


def decode(q_ref, g):
    codes = q_ref[g, GRP : GRP + EXT, :].astype(jnp.int32).astype(F32)[0:1, :]
    code = jnp.sum(jnp.where(eye(GRP), codes, 0.0), axis=1, keepdims=True)
    scale = jnp.exp2(code * (1.0 / CODE)) * (1.0 / TOP)
    return q_ref[g, 0:GRP, :].astype(jnp.int32).astype(F32) * scale


def stash(f, k, at, high_ref, low_ref):
    high, low = halves(f)
    high_ref[at, k * KP : (k + 1) * KP] = high
    low_ref[at, k * KP : (k + 1) * KP] = low


def schur_kernel(
    rows_ref, cols_ref, order_ref, starts_ref, member_ref, front_ref, tiles_ref, *refs, count
):
    own, mine, other = refs[:count], refs[count : 2 * count], refs[2 * count : 3 * count]
    f_ref, out_ref, fh_ref, fl_ref, sh_ref, sl_ref = refs[3 * count :]
    tile = tiles_ref.shape[1]
    i, j = pl.program_id(0), pl.program_id(1)
    groups = mine[0].shape[0]

    @pl.when((i == 0) & (j == 0))
    def _():
        def step(g, carry):
            for e, strip in enumerate((mine, other)):
                member = member_ref[0] if e == 0 else 1 - member_ref[0]
                at = pl.ds(pl.multiple_of((member * groups + g) * GRP, GRP), GRP)
                for k in range(count):
                    stash(decode(strip[k], g), k, at, sh_ref, sl_ref)
            return carry

        lax.fori_loop(0, groups, step, 0)

    @pl.when(j == 0)
    def _():
        def step(g, carry):
            at = pl.ds(pl.multiple_of(g * GRP, GRP), GRP)
            for k in range(count):
                f = decode(own[k], g)
                f_ref[at, k * KP : (k + 1) * KP] = f
                stash(f, k, at, fh_ref, fl_ref)
            return carry

        lax.fori_loop(0, own[0].shape[0], step, 0)

    high, wide = out_ref.shape
    at = pl.ds(pl.multiple_of(j * wide, wide), wide)
    prod = dot_halves((fh_ref[...], fl_ref[...]), (sh_ref[at, :], sl_ref[at, :]))
    out_ref[...] = front_ref[...] - prod
    block = i * pl.num_programs(1) + j
    scalars = (rows_ref, cols_ref, order_ref, starts_ref)
    add_tiles(scalars, tiles_ref, out_ref, block, i * (high // tile), j * (wide // tile))


def schur(place_rows, place_cols, member, front, tiles, own, mine, other):
    rows, cols = front.shape
    tile = tiles.shape[1]
    count = len(own)
    once = pl.Buffered(1)
    high, wide = min(rows, 1024), min(cols, 512)
    depth = count * KP
    order, starts = bucket(
        place_rows, place_cols, high // tile, wide // tile, rows // high, cols // wide
    )
    block = pl.BlockSpec((high, wide), lambda i, j, *_: (i, j))
    coded = pl.BlockSpec((high // GRP, GRP + EXT, KP), lambda i, j, *_: (i, 0, 0))
    strip = pl.BlockSpec(mine[0].shape, lambda i, j, *_: (0, 0, 0), pipeline_mode=once)
    return pl.pallas_call(
        functools.partial(schur_kernel, count=count),
        out_shape=[jax.ShapeDtypeStruct((rows, PW), F32), jax.ShapeDtypeStruct((rows, cols), F32)],
        grid_spec=pltpu.PrefetchScalarGridSpec(
            num_scalar_prefetch=5,
            grid=(rows // high, cols // wide),
            in_specs=[block, pl.BlockSpec(tiles.shape, lambda i, j, *_: (0, 0, 0), pipeline_mode=once)]
            + [coded] * count
            + [strip] * (2 * count),
            out_specs=[pl.BlockSpec((high, depth), lambda i, j, *_: (i, 0)), block],
            scratch_shapes=[pltpu.VMEM((high, depth), jnp.bfloat16)] * 2
            + [pltpu.VMEM((cols, depth), jnp.bfloat16)] * 2,
        ),
        compiler_params=params(),
        name="schur",
    )(place_rows, place_cols, order, starts, member, front, tiles, *own, *mine, *other)


def gray(n):
    return [i ^ (i >> 1) for i in range(n)]


def ring_pairs(row_count, col_count, hop, turn):
    chips = row_count // 2
    order = gray(chips)
    pairs = []
    for col in range(col_count):
        at = order.index(col)
        for member in range(2):
            way = turn if member == 0 else -turn
            src = order[(at + way * (hop - 1)) % chips] * 2 + member
            dst = order[(at + way * hop) % chips] * 2 + member
            pairs.append((src * col_count + col, dst * col_count + col))
    return pairs


def body(front_init, child_tiles, child_dest):
    row_count = lax.axis_size("row")
    col_count = lax.axis_size("col")
    if row_count != 2 * col_count:
        raise ValueError("mesh shape")
    row_extent, col_extent = front_init.shape
    tile_width = child_tiles.shape[1]
    tile_grid = col_extent * col_count // tile_width
    row_tiles = row_extent // tile_width
    col_tiles = col_extent // tile_width
    tile_count = child_tiles.shape[0]
    row_index = lax.axis_index("row")
    col_index = lax.axis_index("col")

    tile_row = child_dest // tile_grid
    tile_col = child_dest % tile_grid
    owner_row = tile_row // row_tiles
    local_tile = (tile_row - owner_row * row_tiles) * col_tiles + (tile_col - col_index * col_tiles)
    positions = jnp.arange(tile_count)
    earlier = positions[None, :] < positions[:, None]
    same_owner = owner_row[:, None] == owner_row[None, :]
    send_rank = jnp.sum((same_owner & earlier).astype(jnp.int32), axis=1)
    send_slot = owner_row * CAP + send_rank
    slots = jnp.arange(row_count * CAP)
    hit = slots[:, None] == send_slot[None, :]
    index = jnp.sum(jnp.where(hit, positions[None, :], 0), axis=1).astype(jnp.int32)
    targets = jnp.sum(jnp.where(hit, local_tile[None, :] + 1, 0), axis=1).astype(jnp.int32) - 1
    places = lax.all_to_all(targets, "row", split_axis=0, concat_axis=0, tiled=True)
    place_rows = jnp.where(places < 0, -1, places // col_tiles)
    place_cols = places % col_tiles

    both = ("row", "col")
    chips = row_count // 2
    member = row_index % 2
    order = jnp.array(gray(chips))
    here = jnp.argmax(order == row_index // 2)
    there = jnp.argmax(order == col_index)
    distance = jnp.where(member == 0, here - there, there - here) % chips
    swap = [(r * col_count + c, (r ^ 1) * col_count + c) for r in range(row_count) for c in range(col_count)]

    outgoing = pack(index, child_tiles)
    arrived = lax.all_to_all(outgoing, "row", split_axis=0, concat_axis=0, tiled=True)

    count = PW // KP
    at_first = (col_index == 0).astype(jnp.int32)
    row = jnp.stack([row_index.astype(jnp.int32), at_first])
    active = at_first.reshape(1)
    root = active * (row_index == 0).astype(jnp.int32)
    own, mine, other, factors, lowers = [], [], [], [], []
    first, trail = chol_first(root, place_rows, place_cols, front_init, arrived)
    panel_sum = panel(active, place_rows, place_cols, front_init, arrived)
    rest = chol_rest(root, trail)

    def share(low):
        even = [low]
        for chip in range(1, chips):
            pair = (2 * above(chip) * col_count, 2 * chip * col_count)
            even.append(lax.ppermute(even[above(chip)], both, [pair]))
        held = []
        for chip in range(chips):
            pair = (2 * chip * col_count, (2 * chip + 1) * col_count)
            held += [even[chip], lax.ppermute(even[chip], both, [pair])]
        return held

    shared = [share(first), share(rest)]
    for k in range(count):
        held = shared[min(k, 1)]
        factor, coded, lower = solve(row, panel_sum, factors, lowers, held)
        factors.append(factor)
        lowers.append(lower)
        steps = [coded]
        for hop in range(col_count - 1):
            steps.append(lax.ppermute(steps[-1], "col", [(hop, hop + 1)]))
        own.append(pick(col_index, steps))
        ahead, back = [own[-1]], [own[-1]]
        for hop in range(1, chips // 2 + 1):
            ahead.append(lax.ppermute(ahead[-1], both, ring_pairs(row_count, col_count, hop, 1)))
        for hop in range(1, chips - chips // 2):
            back.append(lax.ppermute(back[-1], both, ring_pairs(row_count, col_count, hop, -1)))
        mine.append(pick(distance, ahead + back[:0:-1]))
        other.append(lax.ppermute(mine[-1], both, swap))

    member = member.reshape(1).astype(jnp.int32)
    panel_factor, schur_update = schur(
        place_rows, place_cols, member, front_init, arrived, own, mine, other
    )
    return (panel_factor, schur_update)


def above(chip):
    return chip - (1 << (chip.bit_length() - 1))


def solution(mesh):
    return jax.shard_map(
        body,
        mesh=mesh,
        in_specs=(P("row", "col"), P(("row", "col"), None, None), P(("row", "col"))),
        out_specs=(P("row", None), P("row", "col")),
        check_vma=False,
    )
```
